256 devices in a mesh: ctx: 32 (over y, z_lo, core), tp: 8 (over x, z_hi).
Axes of the slice: x: 4, y: 4, z: 8 (z_hi: 2, z_lo: 4; z = z_hi * 4 + z_lo), core: 2. Of those that a mesh axis runs over, the one named last changes fastest.
Arguments:
- tokens: bfloat16 [12288, 3072], P('ctx', 'tp'), may hold values from -6 to 6
- queries: bfloat16 [12288, 2048], P('ctx', 'tp'), may hold values from -16 to 16
- key_rows: bfloat16 [12288, 2048], P('ctx', 'tp'), may hold values from -16 to 16
- value_rows: bfloat16 [12288, 2048], P('ctx', 'tp'), may hold values from -6 to 6
- clip_ids: int32 [12288], replicated, may hold values from 0 to 3, never falling along the last dimension, each value on 1 to 9216 neighbouring positions
- causal: int32 [4], replicated, may hold values 0 or 1
- modulation: float32 [3, 4, 3072], replicated, may hold values from -3 to 3
- w_mlp: bfloat16 [3072, 6144], P(None, 'tp'), may hold values from -0.109375 to 0.109375
- w_attn_out: bfloat16 [2048, 3072], P('tp'), may hold values from -1 to 1
- w_mlp_out: bfloat16 [6144, 3072], P('tp'), may hold values from -0.078125 to 0.078125
Outputs:
- mixed: float32 [12288, 3072], P(('ctx', 'tp'))
The draws below stay inside these ranges and needn't reach their ends.
Inputs may be any that keep to these rules, and one draw needn't show every extreme that they name: `clip_ids`: clip numbers never fall along the tokens; each of the 4 clips has 1 to 9216 tokens and one has exactly 9216.
All inputs are finite; a program needn't handle non-finite values.
Results may differ from the reference program's by a relative error of at most 0.0065.
Values may be sent and summed in bfloat16 or wider, within the bound.
A program may use at most 128 MiB of HBM per device.

```python
import math
import jax
import jax.numpy as jnp
import numpy as np
from jax import lax

D = 3072
HEADS = 16
HD = 128
MLP = 6144
CLIPS = 4
TOKENS = 12288
MOST = 9216


def draw_queries(key, part):
    drawn_rows = jnp.clip(jax.random.normal(jax.random.fold_in(key, 1), (TOKENS, HEADS * HD), jnp.float32), -4.0, 4.0)
    return drawn_rows.astype(jnp.bfloat16)


def draw_key_rows(key, part):
    drawn_rows = jnp.clip(jax.random.normal(jax.random.fold_in(key, 2), (TOKENS, HEADS * HD), jnp.float32), -4.0, 4.0)
    return drawn_rows.astype(jnp.bfloat16)


def touch_ends(result, rng, low, largest):
    shape = result.shape
    index_at = [jax.random.randint(jax.random.fold_in(rng, axis), (), 0, shape[axis]) for axis in range(len(shape))]
    result = result.at[tuple(index_at)].set(low)
    longest = shape.index(max(shape))
    index_at[longest] = (index_at[longest] + 1) % shape[longest]
    return result.at[tuple(index_at)].set(largest)


def shard_levels(key, shape, shards, smallest, top_value):
    loudness = 1.0
    for axis_at, blocks in shards:
        steps = jax.random.uniform(jax.random.fold_in(jax.random.fold_in(key, 6), axis_at), (blocks,), jnp.float32, smallest / len(shards), top_value / len(shards))
        loudness = loudness * jnp.repeat(jnp.exp(steps), shape[axis_at] // blocks).reshape((-1,) + (1,) * (len(shape) - 1 - axis_at))
    return loudness


def split_up(amount, total, limit, lean):
    weights = [(1 << 20) // math.isqrt(standing ** lean) + 1 for standing in range(2, amount + 1)]
    surplus, counts = total - limit - (amount - 1), [1] * (amount - 1)
    while surplus > 0:
        candidates = [i for i in range(amount - 1) if counts[i] < limit]
        pool, budget = sum([weights[i] for i in candidates]), surplus
        for i in candidates:
            extra = min(limit - counts[i], max(1, budget * weights[i] // pool), surplus)
            counts[i] = counts[i] + extra
            surplus = surplus - extra
    return np.array([limit] + counts)


def uneven_parts(rng, amount, total, most, lean):
    if amount == 2:
        one = jax.random.randint(rng, (), max(1, total - most), min(most, total - 1) + 1)
        return jnp.stack([one, total - one])
    lengths = jnp.asarray(split_up(amount, total, most, lean), jnp.int32)
    pairs = (amount - 1) // 2
    donor, taker = lengths[1:1 + 2 * pairs:2], lengths[2:2 + 2 * pairs:2]
    slack = jnp.minimum(donor - 1, most - taker)
    passed = jax.random.randint(jax.random.fold_in(rng, 1), (pairs,), 0, 1 << 20) % (slack + 1)
    lengths = lengths.at[1:1 + 2 * pairs:2].set(donor - passed).at[2:2 + 2 * pairs:2].set(taker + passed)
    return lengths[jax.random.permutation(jax.random.fold_in(rng, 2), amount)]


def bell_draw(rng, shape, width, reach, shards=(), kind=jnp.bfloat16):
    result = jax.random.normal(rng, shape, jnp.float32) * width
    if len(shards) > 0:
        result = shard_levels(rng, shape, shards, -0.22, 0.18) * result
    return jnp.clip(result, min=-reach, max=reach).astype(kind)


def setup_inputs(seed: int = 0) -> dict:
    key_list = jax.random.split(jax.random.key(seed), 11)
    tokens = bell_draw(key_list[0], (TOKENS, D), 1.0, 6.0, ((0, 32), (1, 8)))
    queries = draw_queries(jax.random.fold_in(key_list[10], 71), 0)
    key_rows = draw_key_rows(jax.random.fold_in(key_list[10], 71), 0)
    value_rows = bell_draw(key_list[3], (TOKENS, HEADS * HD), 1.0, 6.0, ((0, 32), (1, 8)))
    clip_ids = jnp.searchsorted(jnp.cumsum(uneven_parts(key_list[4], CLIPS, TOKENS, MOST, 0)), jnp.arange(TOKENS), side="right").astype(jnp.int32)
    causal = touch_ends((jax.random.randint(key_list[5], (CLIPS,), 0, 2) < 1).astype(jnp.int32), jax.random.fold_in(key_list[5], 1), 0, 1)
    modulation = bell_draw(key_list[6], (3, CLIPS, D), 0.5, 3.0, (), jnp.float32)
    w_mlp = bell_draw(key_list[7], (D, MLP), D ** -0.5, 0.109375, ((1, 8),))
    w_attn_out = bell_draw(key_list[8], (HEADS * HD, D), (HEADS * HD // 64) ** -0.5, 1.0, ((0, 8),))
    w_mlp_out = bell_draw(key_list[9], (MLP, D), MLP ** -0.5, 0.078125, ((0, 8),))
    return {"tokens": tokens, "queries": queries, "key_rows": key_rows, "value_rows": value_rows, "clip_ids": clip_ids, "causal": causal, "modulation": modulation, "w_mlp": w_mlp, "w_attn_out": w_attn_out, "w_mlp_out": w_mlp_out}


neg_large = -1e+30
eps_norm = 1e-06

def attention(queries, key_rows, value_rows, clip_ids, causal):
    tile_width = math.gcd(TOKENS, 256)
    blocks = TOKENS // tile_width
    inverse_root = 1.0 / math.sqrt(HD)
    key_all = key_rows.astype(jnp.float32).reshape(TOKENS, HEADS, HD)
    value_all = value_rows.astype(jnp.float32).reshape(TOKENS, HEADS, HD)
    positions = jnp.arange(TOKENS, dtype=jnp.int32)
    causal_tok = causal[clip_ids]

    def one_block(tile_items):
        query_tile, pos_tile, id_tile, causal_tile = tile_items
        scores = jnp.einsum('ihd,jhd->hij', query_tile.astype(jnp.float32), key_all, precision=lax.Precision.HIGHEST) * inverse_root
        allowed = (id_tile[:, None] == clip_ids[None, :]) & ((causal_tile[:, None] == 0) | (positions[None, :] <= pos_tile[:, None]))
        scores = jnp.where(allowed[None], scores, neg_large)
        row_peak = lax.optimization_barrier(jnp.max(scores, axis=2, keepdims=True))
        weights = jnp.where(allowed[None], jnp.exp(scores - row_peak), 0.0).astype(jnp.bfloat16)
        weights = lax.optimization_barrier(weights).astype(jnp.float32)
        numerator = jnp.einsum('hij,jhd->ihd', weights, value_all, precision=lax.Precision.HIGHEST)
        denominator = jnp.transpose(lax.optimization_barrier(jnp.sum(weights, axis=2)))
        return (numerator / denominator[:, :, None]).astype(jnp.bfloat16).reshape(tile_width, HEADS * HD)
    attended_tiles = lax.map(one_block, (queries.reshape(blocks, tile_width, HEADS, HD), positions.reshape(blocks, tile_width), clip_ids.reshape(blocks, tile_width), causal_tok.reshape(blocks, tile_width)))
    return attended_tiles.reshape(TOKENS, HEADS * HD)

def reference(tokens, queries, key_rows, value_rows, clip_ids, causal, modulation, w_mlp, w_attn_out, w_mlp_out):
    token_values = tokens.astype(jnp.float32)
    row_mean = lax.optimization_barrier(jnp.mean(token_values, axis=1, keepdims=True))
    centred = token_values - row_mean
    row_var = lax.optimization_barrier(jnp.mean(centred * centred, axis=1, keepdims=True))
    normed = centred * lax.rsqrt(row_var + eps_norm)
    shift_rows = modulation[0][clip_ids]
    scale_rows = modulation[1][clip_ids]
    gate_rows = modulation[2][clip_ids]
    modulated = (normed * (1.0 + scale_rows) + shift_rows).astype(jnp.bfloat16)
    hidden = jax.nn.gelu(jnp.dot(modulated, w_mlp, preferred_element_type=jnp.float32), approximate=True).astype(jnp.bfloat16)
    attended = attention(queries, key_rows, value_rows, clip_ids, causal)
    branch = jnp.dot(attended, w_attn_out, preferred_element_type=jnp.float32) + jnp.dot(hidden, w_mlp_out, preferred_element_type=jnp.float32)
    return token_values + gate_rows * branch
```

```python
import functools
import math

import jax
import jax.numpy as jnp
from jax import lax
from jax.experimental import pallas as pl
from jax.experimental.pallas import tpu as pltpu
from jax.sharding import PartitionSpec as P

HD = 128
TILE = 1024
neg_large = -1e30
eps_norm = 1e-06


def pick_rows(clip_rows, table):
    out = jnp.broadcast_to(table[0][None, :], (clip_rows.shape[0], table.shape[1]))
    for clip in range(1, table.shape[0]):
        out = jnp.where(clip_rows[:, None] == clip, table[clip][None, :], out)
    return out


def attend_kernel(bounds, q_ref, start_ref, end_ref, k_ref, v_ref, out_ref, acc, peak):
    step = pl.program_id(0)
    tile = bounds[0] + step
    factor = math.log2(math.e) / math.sqrt(HD)
    heads = q_ref.shape[1] // HD

    @pl.when(step == 0)
    def _():
        acc[...] = jnp.zeros_like(acc)
        peak[...] = jnp.full_like(peak, neg_large)

    def one_tile(masked):
        rows = q_ref.shape[0]
        if masked:
            pos = tile * TILE + lax.broadcasted_iota(jnp.int32, (rows, TILE), 1)
            allowed = (pos >= start_ref[...]) & (pos < end_ref[...])
        ones = jnp.ones((TILE, HD), jnp.bfloat16)
        for head in range(heads):
            cols = slice(head * HD, (head + 1) * HD)
            scores = lax.dot_general(
                q_ref[:, cols], k_ref[:, cols], (((1,), (1,)), ((), ())),
                preferred_element_type=jnp.float32,
            )
            if masked:
                scores = jnp.where(allowed, scores, neg_large)
            old = peak[head]
            new = jnp.maximum(old, jnp.max(scores, axis=1, keepdims=True))
            weights = jnp.exp2((scores - new[:, :1]) * factor)
            if masked:
                weights = jnp.where(allowed, weights, 0.0)
            shrink = jnp.exp2((old - new) * factor)
            values = jnp.concatenate([v_ref[:, cols], ones], axis=1)
            added = jnp.dot(
                weights.astype(jnp.bfloat16), values, preferred_element_type=jnp.float32
            )
            acc[head] = acc[head] * jnp.concatenate([shrink, shrink], axis=1) + added
            peak[head] = new

    active = tile < bounds[1]
    whole = (tile >= bounds[2]) & (tile < bounds[3])

    @pl.when(active & whole)
    def _():
        one_tile(False)

    @pl.when(active & jnp.logical_not(whole))
    def _():
        one_tile(True)

    @pl.when(step == pl.num_programs(0) - 1)
    def _():
        for head in range(heads):
            out_ref[:, head * HD:(head + 1) * HD] = (
                acc[head][:, :HD] / acc[head][:, HD:]
            ).astype(out_ref.dtype)


def attention(queries, keys, values, row_start, row_end):
    rows, width = queries.shape
    tiles = keys.shape[0] // TILE
    low = jnp.min(row_start) // TILE
    high = (jnp.max(row_end) + TILE - 1) // TILE
    whole_low = (jnp.max(row_start) + TILE - 1) // TILE
    whole_high = jnp.min(row_end) // TILE
    bounds = jnp.stack([low, high, whole_low, whole_high]).astype(jnp.int32)

    def kv_map(step, bounds):
        return (jnp.minimum(bounds[0] + step, bounds[1] - 1), 0)

    def fixed(step, bounds):
        return (0, 0)

    return pl.pallas_call(
        attend_kernel,
        out_shape=jax.ShapeDtypeStruct((rows, width), jnp.bfloat16),
        grid_spec=pltpu.PrefetchScalarGridSpec(
            num_scalar_prefetch=1,
            grid=(tiles,),
            in_specs=[
                pl.BlockSpec((rows, width), fixed),
                pl.BlockSpec((rows, 1), fixed),
                pl.BlockSpec((rows, 1), fixed),
                pl.BlockSpec((TILE, width), kv_map),
                pl.BlockSpec((TILE, width), kv_map),
            ],
            out_specs=pl.BlockSpec((rows, width), fixed),
            scratch_shapes=[
                pltpu.VMEM((width // HD, rows, 2 * HD), jnp.float32),
                pltpu.VMEM((width // HD, rows, HD), jnp.float32),
            ],
        ),
        compiler_params=pltpu.CompilerParams(vmem_limit_bytes=40 << 20),
        name="attend",
    )(bounds, queries, row_start[:, None], row_end[:, None], keys, values)


def per_device(
    tokens, queries, key_rows, value_rows, clip_ids, causal, modulation, w_mlp, w_attn_out, w_mlp_out
):
    local_rows = queries.shape[0]
    tp_size = lax.axis_size("tp")
    clips = causal.shape[0]
    first_row = lax.axis_index("ctx") * local_rows
    own_pos = first_row + jnp.arange(local_rows, dtype=jnp.int32)
    own_ids = lax.dynamic_slice_in_dim(clip_ids, first_row, local_rows)
    key_all = lax.all_gather(key_rows, "ctx", axis=0, tiled=True)
    value_all = lax.all_gather(value_rows, "ctx", axis=0, tiled=True)

    numbers = jnp.arange(clips, dtype=jnp.int32)
    clip_start = jnp.sum((clip_ids[None, :] < numbers[:, None]).astype(jnp.int32), axis=1)
    clip_end = jnp.sum((clip_ids[None, :] <= numbers[:, None]).astype(jnp.int32), axis=1)
    mine = own_ids[:, None] == numbers[None, :]
    row_start = jnp.sum(jnp.where(mine, clip_start[None, :], 0), axis=1)
    row_end = jnp.sum(jnp.where(mine, clip_end[None, :], 0), axis=1)
    row_causal = jnp.sum(jnp.where(mine, causal[None, :], 0), axis=1)
    row_end = jnp.where(row_causal == 0, row_end, own_pos + 1)

    whole_rows = lax.all_gather(tokens, "tp", axis=1, tiled=True)
    token_values = whole_rows.astype(jnp.float32)
    row_mean = jnp.mean(token_values, axis=1, keepdims=True)
    centred = token_values - row_mean
    row_var = jnp.mean(centred * centred, axis=1, keepdims=True)
    normed = centred * lax.rsqrt(row_var + eps_norm)
    shift_rows = pick_rows(own_ids, modulation[0])
    scale_rows = pick_rows(own_ids, modulation[1])
    modulated = (normed * (1.0 + scale_rows) + shift_rows).astype(jnp.bfloat16)
    hidden = jax.nn.gelu(
        jnp.dot(modulated, w_mlp, preferred_element_type=jnp.float32), approximate=True
    ).astype(jnp.bfloat16)

    attended = attention(queries, key_all, value_all, row_start, row_end)
    part = jnp.dot(attended, w_attn_out, preferred_element_type=jnp.float32) + jnp.dot(
        hidden, w_mlp_out, preferred_element_type=jnp.float32
    )
    branch = lax.psum_scatter(
        part.astype(jnp.bfloat16), "tp", scatter_dimension=0, tiled=True
    ).astype(jnp.float32)
    share_rows = local_rows // tp_size
    first_share = lax.axis_index("tp") * share_rows
    share_ids = lax.dynamic_slice_in_dim(own_ids, first_share, share_rows)
    residual = lax.dynamic_slice_in_dim(whole_rows, first_share, share_rows, 0).astype(jnp.float32)
    return residual + pick_rows(share_ids, modulation[2]) * branch


def solution(mesh):
    in_specs = (
        P("ctx", "tp"), P("ctx", "tp"), P("ctx", "tp"), P("ctx", "tp"),
        P(), P(), P(), P(None, "tp"), P("tp", None), P("tp", None),
    )
    out_specs = P(("ctx", "tp"), None)
    return jax.shard_map(
        per_device, mesh=mesh, in_specs=in_specs, out_specs=out_specs, check_vma=False
    )
```

```python
import math

import jax
import jax.numpy as jnp
from jax import lax
from jax.experimental import pallas as pl
from jax.experimental.pallas import tpu as pltpu
from jax.sharding import PartitionSpec as P

HD = 128
TILE = 1024
neg_large = -1e30
eps_norm = 1e-06


def pick_rows(clip_rows, table):
    out = jnp.broadcast_to(table[0][None, :], (clip_rows.shape[0], table.shape[1]))
    for clip in range(1, table.shape[0]):
        out = jnp.where(clip_rows[:, None] == clip, table[clip][None, :], out)
    return out


def attend_kernel(bounds, q_ref, start_ref, end_ref, k_ref, v_ref, out_ref, acc, peak):
    step = pl.program_id(0)
    tile = bounds[0] + step
    factor = math.log2(math.e) / math.sqrt(HD)
    heads = q_ref.shape[1] // HD

    @pl.when(step == 0)
    def _():
        acc[...] = jnp.zeros_like(acc)
        peak[...] = jnp.full_like(peak, neg_large)

    def one_tile(masked):
        rows = q_ref.shape[0]
        if masked:
            pos = tile * TILE + lax.broadcasted_iota(jnp.int32, (rows, TILE), 1)
            allowed = (pos >= start_ref[...]) & (pos < end_ref[...])
        ones = jnp.ones((TILE, HD), jnp.bfloat16)
        for head in range(heads):
            cols = slice(head * HD, (head + 1) * HD)
            scores = lax.dot_general(
                q_ref[:, cols], k_ref[:, cols], (((1,), (1,)), ((), ())),
                preferred_element_type=jnp.float32,
            )
            if masked:
                scores = jnp.where(allowed, scores, neg_large)
            old = peak[head]
            new = jnp.maximum(old, jnp.max(scores, axis=1, keepdims=True))
            weights = jnp.exp2((scores - new[:, :1]) * factor)
            if masked:
                weights = jnp.where(allowed, weights, 0.0)
            shrink = jnp.exp2((old - new) * factor)
            values = jnp.concatenate([v_ref[:, cols], ones], axis=1)
            added = jnp.dot(
                weights.astype(jnp.bfloat16), values, preferred_element_type=jnp.float32
            )
            acc[head] = acc[head] * jnp.concatenate([shrink, shrink], axis=1) + added
            peak[head] = new

    active = tile < bounds[1]
    whole = (tile >= bounds[2]) & (tile < bounds[3])

    @pl.when(active & whole)
    def _():
        one_tile(False)

    @pl.when(active & jnp.logical_not(whole))
    def _():
        one_tile(True)

    @pl.when(step == pl.num_programs(0) - 1)
    def _():
        for head in range(heads):
            out_ref[:, head * HD:(head + 1) * HD] = (
                acc[head][:, :HD] / acc[head][:, HD:]
            ).astype(out_ref.dtype)


def attention(queries, keys, values, row_start, row_end):
    rows, width = queries.shape
    tiles = keys.shape[0] // TILE
    low = jnp.min(row_start) // TILE
    high = (jnp.max(row_end) + TILE - 1) // TILE
    whole_low = (jnp.max(row_start) + TILE - 1) // TILE
    whole_high = jnp.min(row_end) // TILE
    bounds = jnp.stack([low, high, whole_low, whole_high]).astype(jnp.int32)

    def kv_map(step, bounds):
        return (jnp.minimum(bounds[0] + step, bounds[1] - 1), 0)

    def fixed(step, bounds):
        return (0, 0)

    return pl.pallas_call(
        attend_kernel,
        out_shape=jax.ShapeDtypeStruct((rows, width), jnp.bfloat16),
        grid_spec=pltpu.PrefetchScalarGridSpec(
            num_scalar_prefetch=1,
            grid=(tiles,),
            in_specs=[
                pl.BlockSpec((rows, width), fixed),
                pl.BlockSpec((rows, 1), fixed),
                pl.BlockSpec((rows, 1), fixed),
                pl.BlockSpec((TILE, width), kv_map),
                pl.BlockSpec((TILE, width), kv_map),
            ],
            out_specs=pl.BlockSpec((rows, width), fixed),
            scratch_shapes=[
                pltpu.VMEM((width // HD, rows, 2 * HD), jnp.float32),
                pltpu.VMEM((width // HD, rows, HD), jnp.float32),
            ],
        ),
        compiler_params=pltpu.CompilerParams(vmem_limit_bytes=40 << 20),
        cost_estimate=pl.CostEstimate(
            flops=8 * rows * keys.shape[0] * width,
            bytes_accessed=4 * keys.shape[0] * width,
            transcendentals=rows * keys.shape[0] * width // HD,
        ),
        name="attend",
    )(bounds, queries, row_start[:, None], row_end[:, None], keys, values)


def remote(src, dst, send_sem, recv_sem, where):
    return pltpu.make_async_remote_copy(
        src_ref=src, dst_ref=dst, send_sem=send_sem, recv_sem=recv_sem,
        device_id=where, device_id_type=pl.DeviceIdType.MESH,
    )


def greet(places):
    barrier = pltpu.get_barrier_semaphore()
    for place in places:
        pl.semaphore_signal(
            barrier, inc=1, device_id=place, device_id_type=pl.DeviceIdType.MESH
        )
    pl.semaphore_wait(barrier, len(places))


Y, Z, CORES = 4, 4, 2
KV_COPIES = 2 * (Z - 1) + 6 * Z + 2 * Y * Z


def gather_kernel(keys, values, key_all, value_all, send, recv, local):
    rows = keys.shape[0]
    me = lax.axis_index("ctx")
    y, z, core = me // (Z * CORES), me // CORES % Z, me % CORES
    pair = (key_all, value_all)
    own = (keys, values)

    def index(dy, dz, flip=False):
        other = 1 - core if flip else core
        return ((y + dy + Y) % Y * Z + (z + dz + Z) % Z) * CORES + other

    def slot(which, dy, dz, flip=False):
        start = pl.multiple_of(index(dy, dz, flip) * rows, rows)
        return pair[which].at[pl.ds(start, rows)]

    def at(dy, dz, flip=False):
        return {"ctx": index(dy, dz, flip)}

    greet([at(0, d) for d in range(1, Z)] + [at(1, 0), at(-1, 0), at(0, 0, True)])
    started = []
    made = [0]

    def make(src, which, owner, target):
        number = made[0]
        made[0] += 1
        copy = remote(
            src, slot(which, *owner), send.at[number], recv.at[number], at(*target)
        )
        copy.start()
        started.append(copy)
        return copy

    stay = [pltpu.make_async_copy(own[w], slot(w, 0, 0), local.at[w]) for w in (0, 1)]
    for copy in stay:
        copy.start()
    near = [[None] * 4 for _ in range(Z)]
    far = [[None] * 2 for _ in range(Z)]
    to_z = [[None] * 2 for _ in range(Z)]
    to_core = []

    def spread(dz):
        for w in (0, 1):
            src = own[w] if dz == 0 else slot(w, 0, dz)
            near[dz][w] = make(src, w, (0, dz), (1, 0))
            near[dz][2 + w] = make(src, w, (0, dz), (-1, 0))
            to_core.append(make(src, w, (0, dz), (0, 0, True)))

    def relay(dz):
        near[dz][0].wait_recv()
        far[dz][0] = make(slot(0, -1, dz), 0, (-1, dz), (1, 0))
        near[dz][3].wait_recv()
        far[dz][1] = make(slot(1, 1, dz), 1, (1, dz), (-1, 0))
        near[dz][1].wait_recv()
        near[dz][2].wait_recv()
        for w in (0, 1):
            for dy in (-1, 1):
                to_core.append(make(slot(w, dy, dz), w, (dy, dz), (0, 0, True)))

    def finish(dz):
        for w in (0, 1):
            far[dz][w].wait_recv()
            to_core.append(make(slot(w, 2, dz), w, (2, dz), (0, 0, True)))

    for d in (1, 3, 2):
        for w in (0, 1):
            to_z[Z - d][w] = make(own[w], w, (0, 0), (0, d))
    spread(0)
    order = (0, 1, 3, 2)
    for i, dz in enumerate(order):
        if i > 0:
            for w in (0, 1):
                to_z[dz][w].wait_recv()
            spread(dz)
            relay(order[i - 1])
        if i > 1:
            finish(order[i - 2])
    relay(order[Z - 1])
    finish(order[Z - 2])
    finish(order[Z - 1])
    for copy in to_core:
        copy.wait_recv()
    for copy in started:
        copy.wait_send()
    for copy in stay:
        copy.wait()


def gather_rows(keys, values, devices):
    rows, width = keys.shape
    hbm = pl.BlockSpec(memory_space=pl.ANY)
    whole = jax.ShapeDtypeStruct((rows * devices, width), keys.dtype)
    return pl.pallas_call(
        gather_kernel,
        out_shape=(whole, whole),
        in_specs=[hbm, hbm],
        out_specs=(hbm, hbm),
        scratch_shapes=[
            pltpu.SemaphoreType.DMA((KV_COPIES,)),
            pltpu.SemaphoreType.DMA((KV_COPIES,)),
            pltpu.SemaphoreType.DMA((2,)),
        ],
        compiler_params=pltpu.CompilerParams(collective_id=0, has_side_effects=True),
        cost_estimate=pl.CostEstimate(flops=0, bytes_accessed=150_000_000, transcendentals=0),
        name="gather_kv",
    )(keys, values)


X, HI, CHUNKS = 4, 2, 4


def reduce_kernel(part, out, held, relayed, outgoing, incoming, sums, send, recv):
    rows = part.shape[0] // (X * HI)
    wide = part.shape[1] // CHUNKS
    me = lax.axis_index("tp")
    x, hi = me // HI, me % HI
    right = {"tp": (x + 1) % X * HI + hi}
    left = {"tp": (x + X - 1) % X * HI + hi}
    across = {"tp": x * HI + 1 - hi}
    greet([left, right, across])

    def piece(dx, first, count, chunk):
        start = pl.multiple_of(((x + dx) % X * HI + first) * rows, rows)
        return part.at[pl.ds(start, count * rows), pl.ds(chunk * wide, wide)]

    def cols(chunk):
        return slice(chunk * wide, (chunk + 1) * wide)

    def copy(src, dst, chunk, kind, where):
        made = remote(src, dst, send.at[chunk, kind], recv.at[chunk, kind], where)
        made.start()
        return made

    copies = [[None] * 7 for _ in range(CHUNKS)]

    def begin(c):
        mine = copies[c]
        mine[2] = copy(piece(2, 0, 1, c), relayed.at[0, c], c, 2, right)
        mine[3] = copy(piece(2, 1, 1, c), relayed.at[1, c], c, 3, left)
        mine[0] = copy(piece(1, 0, 2, c), held.at[0, c], c, 0, right)
        mine[1] = copy(piece(3, 0, 2, c), held.at[1, c], c, 1, left)

    def forward(c):
        mine = copies[c]
        mine[2].wait_recv()
        mine[4] = copy(relayed.at[0, c], held.at[2, c, pl.ds(0, rows)], c, 4, right)
        mine[3].wait_recv()
        mine[5] = copy(relayed.at[1, c], held.at[2, c, pl.ds(rows, rows)], c, 5, left)

    def total(c, half):
        start = pl.multiple_of(half * rows, rows)
        own = pl.multiple_of((x * HI + half) * rows, rows)
        result = part[pl.ds(own, rows), cols(c)].astype(jnp.float32)
        for source in range(3):
            result += held[source, c, pl.ds(start, rows)].astype(jnp.float32)
        return result

    def combine(c):
        mine = copies[c]
        for kind in (0, 1, 4, 5):
            mine[kind].wait_recv()
        outgoing[c] = total(c, 1 - hi).astype(jnp.bfloat16)
        sums[c] = total(c, hi)
        mine[6] = copy(outgoing.at[c], incoming.at[c], c, 6, across)

    for c in range(CHUNKS):
        begin(c)
    for c in range(CHUNKS):
        forward(c)
        if c > 0:
            combine(c - 1)
    combine(CHUNKS - 1)
    for c in range(CHUNKS):
        copies[c][6].wait_recv()
        out[:, cols(c)] = sums[c] + incoming[c].astype(jnp.float32)
    for mine in copies:
        for made in mine:
            made.wait_send()


def reduce_rows(part):
    rows, width = part.shape[0] // (X * HI), part.shape[1]
    wide = width // CHUNKS
    vmem = pl.BlockSpec(memory_space=pltpu.VMEM)
    return pl.pallas_call(
        reduce_kernel,
        out_shape=jax.ShapeDtypeStruct((rows, width), jnp.float32),
        in_specs=[vmem],
        out_specs=vmem,
        scratch_shapes=[
            pltpu.VMEM((3, CHUNKS, HI * rows, wide), jnp.bfloat16),
            pltpu.VMEM((2, CHUNKS, rows, wide), jnp.bfloat16),
            pltpu.VMEM((CHUNKS, rows, wide), jnp.bfloat16),
            pltpu.VMEM((CHUNKS, rows, wide), jnp.bfloat16),
            pltpu.VMEM((CHUNKS, rows, wide), jnp.float32),
            pltpu.SemaphoreType.DMA((CHUNKS, 7)),
            pltpu.SemaphoreType.DMA((CHUNKS, 7)),
        ],
        compiler_params=pltpu.CompilerParams(
            collective_id=1, has_side_effects=True, vmem_limit_bytes=24 << 20
        ),
        cost_estimate=pl.CostEstimate(flops=0, bytes_accessed=100_000_000, transcendentals=0),
        name="reduce_branch",
    )(part)


def per_device(
    tokens, queries, key_rows, value_rows, clip_ids, causal, modulation, w_mlp, w_attn_out, w_mlp_out
):
    local_rows = queries.shape[0]
    tp_size = lax.axis_size("tp")
    clips = causal.shape[0]
    first_row = lax.axis_index("ctx") * local_rows
    own_pos = first_row + jnp.arange(local_rows, dtype=jnp.int32)
    own_ids = lax.dynamic_slice_in_dim(clip_ids, first_row, local_rows)
    key_all, value_all = gather_rows(key_rows, value_rows, lax.axis_size("ctx"))

    numbers = jnp.arange(clips, dtype=jnp.int32)
    clip_start = jnp.sum((clip_ids[None, :] < numbers[:, None]).astype(jnp.int32), axis=1)
    clip_end = jnp.sum((clip_ids[None, :] <= numbers[:, None]).astype(jnp.int32), axis=1)
    mine = own_ids[:, None] == numbers[None, :]
    row_start = jnp.sum(jnp.where(mine, clip_start[None, :], 0), axis=1)
    row_end = jnp.sum(jnp.where(mine, clip_end[None, :], 0), axis=1)
    row_causal = jnp.sum(jnp.where(mine, causal[None, :], 0), axis=1)
    row_end = jnp.where(row_causal == 0, row_end, own_pos + 1)

    whole_rows = lax.all_gather(tokens, "tp", axis=1, tiled=True)
    token_values = whole_rows.astype(jnp.float32)
    row_mean = jnp.mean(token_values, axis=1, keepdims=True)
    centred = token_values - row_mean
    row_var = jnp.mean(centred * centred, axis=1, keepdims=True)
    normed = centred * lax.rsqrt(row_var + eps_norm)
    shift_rows = pick_rows(own_ids, modulation[0])
    scale_rows = pick_rows(own_ids, modulation[1])
    modulated = (normed * (1.0 + scale_rows) + shift_rows).astype(jnp.bfloat16)
    hidden = jax.nn.gelu(
        jnp.dot(modulated, w_mlp, preferred_element_type=jnp.float32), approximate=True
    ).astype(jnp.bfloat16)

    attended = attention(queries, key_all, value_all, row_start, row_end)
    part = jnp.dot(attended, w_attn_out, preferred_element_type=jnp.float32) + jnp.dot(
        hidden, w_mlp_out, preferred_element_type=jnp.float32
    )
    branch = reduce_rows(part.astype(jnp.bfloat16))
    share_rows = local_rows // tp_size
    first_share = lax.axis_index("tp") * share_rows
    share_ids = lax.dynamic_slice_in_dim(own_ids, first_share, share_rows)
    residual = lax.dynamic_slice_in_dim(whole_rows, first_share, share_rows, 0).astype(jnp.float32)
    return residual + pick_rows(share_ids, modulation[2]) * branch


def solution(mesh):
    in_specs = (
        P("ctx", "tp"), P("ctx", "tp"), P("ctx", "tp"), P("ctx", "tp"),
        P(), P(), P(), P(None, "tp"), P("tp", None), P("tp", None),
    )
    out_specs = P(("ctx", "tp"), None)
    return jax.shard_map(
        per_device, mesh=mesh, in_specs=in_specs, out_specs=out_specs, check_vma=False
    )
```

```python
import math

import jax
import jax.numpy as jnp
from jax import lax
from jax.experimental import pallas as pl
from jax.experimental.pallas import tpu as pltpu
from jax.sharding import PartitionSpec as P

HD = 128
TILE = 1024
neg_large = -1e30
eps_norm = 1e-06


def pick_rows(clip_rows, table):
    out = jnp.broadcast_to(table[0][None, :], (clip_rows.shape[0], table.shape[1]))
    for clip in range(1, table.shape[0]):
        out = jnp.where(clip_rows[:, None] == clip, table[clip][None, :], out)
    return out


def interval(table, first, rows):
    clips = table.shape[0] // 2

    def clip_of(pos):
        number = jnp.int32(0)
        for clip in range(clips - 1):
            number = number + (pos >= table[clip]).astype(jnp.int32)
        return number

    def start_of(number):
        return jnp.where(number == 0, 0, table[jnp.maximum(number - 1, 0)])

    low, high = clip_of(first), clip_of(first + rows - 1)
    end = jnp.where(table[clips + high] == 0, table[high], first + rows)
    whole_end = jnp.where(table[clips + low] == 0, table[low], first + 1)
    return start_of(low), end, start_of(high), whole_end


def clips_at(positions, clip_end):
    return jnp.sum((positions[:, None] >= clip_end[None, :-1]).astype(jnp.int32), axis=1)


def attend_kernel(table, q_ref, k_ref, v_ref, out_ref, acc, peak, edges):
    step = pl.program_id(0)
    rows = q_ref.shape[0]
    clips = table.shape[0] // 2
    first = lax.axis_index("ctx") * rows
    some_low, some_high, whole_low, whole_high = interval(table, first, rows)
    tile = some_low // TILE + step
    factor = math.log2(math.e) / math.sqrt(HD)
    heads = q_ref.shape[1] // HD

    @pl.when(step == 0)
    def _():
        acc[...] = jnp.zeros_like(acc)
        peak[...] = jnp.full_like(peak, neg_large)
        pos = first + lax.broadcasted_iota(jnp.int32, (rows, HD), 0)
        start = jnp.zeros_like(pos)
        end = jnp.where(table[clips] == 0, table[0], pos + 1)
        for clip in range(1, clips):
            later = pos >= table[clip - 1]
            start = jnp.where(later, table[clip - 1], start)
            end = jnp.where(
                later, jnp.where(table[clips + clip] == 0, table[clip], pos + 1), end
            )
        edges[0] = start
        edges[1] = end

    def one_tile(masked):
        if masked:
            pos = tile * TILE + lax.broadcasted_iota(jnp.int32, (rows, TILE), 1)
            allowed = (pos >= edges[0][:, :1]) & (pos < edges[1][:, :1])
        ones = jnp.ones((TILE, HD), jnp.bfloat16)
        for head in range(heads):
            cols = slice(head * HD, (head + 1) * HD)
            scores = lax.dot_general(
                q_ref[:, cols], k_ref[:, cols], (((1,), (1,)), ((), ())),
                preferred_element_type=jnp.float32,
            )
            if masked:
                scores = jnp.where(allowed, scores, neg_large)
            old = peak[head]
            new = jnp.maximum(old, jnp.max(scores, axis=1, keepdims=True))
            weights = jnp.exp2((scores - new[:, :1]) * factor)
            if masked:
                weights = jnp.where(allowed, weights, 0.0)
            shrink = jnp.exp2((old - new) * factor)
            values = jnp.concatenate([v_ref[:, cols], ones], axis=1)
            added = jnp.dot(
                weights.astype(jnp.bfloat16), values, preferred_element_type=jnp.float32
            )
            acc[head] = acc[head] * jnp.concatenate([shrink, shrink], axis=1) + added
            peak[head] = new

    active = tile * TILE < some_high
    whole = (tile * TILE >= whole_low) & ((tile + 1) * TILE <= whole_high)

    @pl.when(active & whole)
    def _():
        one_tile(False)

    @pl.when(active & jnp.logical_not(whole))
    def _():
        one_tile(True)

    @pl.when(step == pl.num_programs(0) - 1)
    def _():
        for head in range(heads):
            out_ref[:, head * HD:(head + 1) * HD] = (
                acc[head][:, :HD] / acc[head][:, HD:]
            ).astype(out_ref.dtype)


def attention(queries, keys, values, table):
    rows, width = queries.shape
    tiles = keys.shape[0] // TILE

    def kv_map(step, table):
        low, high, _, _ = interval(table, lax.axis_index("ctx") * rows, rows)
        return (jnp.minimum(low // TILE + step, (high - 1) // TILE), 0)

    def fixed(step, table):
        return (0, 0)

    return pl.pallas_call(
        attend_kernel,
        out_shape=jax.ShapeDtypeStruct((rows, width), jnp.bfloat16),
        grid_spec=pltpu.PrefetchScalarGridSpec(
            num_scalar_prefetch=1,
            grid=(tiles,),
            in_specs=[
                pl.BlockSpec((rows, width), fixed),
                pl.BlockSpec((TILE, width), kv_map),
                pl.BlockSpec((TILE, width), kv_map),
            ],
            out_specs=pl.BlockSpec((rows, width), fixed),
            scratch_shapes=[
                pltpu.VMEM((width // HD, rows, 2 * HD), jnp.float32),
                pltpu.VMEM((width // HD, rows, HD), jnp.float32),
                pltpu.VMEM((2, rows, HD), jnp.int32),
            ],
        ),
        compiler_params=pltpu.CompilerParams(vmem_limit_bytes=60 << 20),
        cost_estimate=pl.CostEstimate(
            flops=8 * rows * keys.shape[0] * width,
            bytes_accessed=4 * keys.shape[0] * width,
            transcendentals=rows * keys.shape[0] * width // HD,
        ),
        name="attend",
    )(table, queries, keys, values)


def remote(src, dst, send_sem, recv_sem, where):
    return pltpu.make_async_remote_copy(
        src_ref=src, dst_ref=dst, send_sem=send_sem, recv_sem=recv_sem,
        device_id=where, device_id_type=pl.DeviceIdType.MESH,
    )


def greet(places):
    barrier = pltpu.get_barrier_semaphore()
    for place in places:
        pl.semaphore_signal(
            barrier, inc=1, device_id=place, device_id_type=pl.DeviceIdType.MESH
        )
    pl.semaphore_wait(barrier, len(places))


Y, Z, CORES = 4, 4, 2
X, HI = 4, 2
COPIES = 2 * (Z - 1) + 6 * Z + 2 * Y * Z + 9


def gather_kernel(tokens, keys, values, whole, key_all, value_all, send, recv, local):
    rows = keys.shape[0]
    me = lax.axis_index("ctx")
    y, z, core = me // (Z * CORES), me // CORES % Z, me % CORES
    pair = (key_all, value_all)
    own = (keys, values)

    def index(dy, dz, flip=False):
        other = 1 - core if flip else core
        return ((y + dy + Y) % Y * Z + (z + dz + Z) % Z) * CORES + other

    def slot(which, dy, dz, flip=False):
        start = pl.multiple_of(index(dy, dz, flip) * rows, rows)
        return pair[which].at[pl.ds(start, rows)]

    def at(dy, dz, flip=False):
        return {"ctx": index(dy, dz, flip)}

    lead = lax.axis_index("tp")
    x, hi = lead // HI, lead % HI
    half, wide = tokens.shape[0] // 2, tokens.shape[1]

    def column(dx, flip=False):
        return (x + dx + X) % X * HI + (1 - hi if flip else hi)

    def strip(dx, flip=False, part=None):
        cols = pl.ds(pl.multiple_of(column(dx, flip) * wide, wide), wide)
        if part is None:
            return whole.at[:, cols]
        return whole.at[pl.ds(part * half, half), cols]

    right, left = {"tp": column(1)}, {"tp": column(-1)}
    across = {"tp": column(0, True)}
    greet(
        [at(0, d) for d in range(1, Z)]
        + [at(1, 0), at(-1, 0), at(0, 0, True), right, left, across]
    )
    started = []
    made = [0]

    def pass_on(src, dst, where):
        number = made[0]
        made[0] += 1
        copy = remote(src, dst, send.at[number], recv.at[number], where)
        copy.start()
        started.append(copy)
        return copy

    over = pass_on(tokens, strip(0), across)
    sides = [pass_on(tokens, strip(0), right), pass_on(tokens, strip(0), left)]

    def make(src, which, owner, target):
        return pass_on(src, slot(which, *owner), at(*target))

    stay = [pltpu.make_async_copy(own[w], slot(w, 0, 0), local.at[w]) for w in (0, 1)]
    stay.append(pltpu.make_async_copy(tokens, strip(0), local.at[2]))
    for copy in stay:
        copy.start()
    near = [[None] * 4 for _ in range(Z)]
    far = [[None] * 2 for _ in range(Z)]
    to_z = [[None] * 2 for _ in range(Z)]
    to_core = []

    def spread(dz):
        for w in (0, 1):
            src = own[w] if dz == 0 else slot(w, 0, dz)
            near[dz][w] = make(src, w, (0, dz), (1, 0))
            near[dz][2 + w] = make(src, w, (0, dz), (-1, 0))
            to_core.append(make(src, w, (0, dz), (0, 0, True)))

    def relay(dz):
        near[dz][0].wait_recv()
        far[dz][0] = make(slot(0, -1, dz), 0, (-1, dz), (1, 0))
        near[dz][3].wait_recv()
        far[dz][1] = make(slot(1, 1, dz), 1, (1, dz), (-1, 0))
        near[dz][1].wait_recv()
        near[dz][2].wait_recv()
        for w in (0, 1):
            for dy in (-1, 1):
                to_core.append(make(slot(w, dy, dz), w, (dy, dz), (0, 0, True)))

    def finish(dz):
        for w in (0, 1):
            far[dz][w].wait_recv()
            to_core.append(make(slot(w, 2, dz), w, (2, dz), (0, 0, True)))

    for d in (1, 3, 2):
        for w in (0, 1):
            to_z[Z - d][w] = make(own[w], w, (0, 0), (0, d))
    spread(0)

    def tokens_far(arrived, flip):
        for copy in arrived:
            copy.wait_recv()
        return [
            pass_on(strip(-1, flip, 0), strip(-1, flip, 0), right),
            pass_on(strip(1, flip, 1), strip(1, flip, 1), left),
        ]

    ends = tokens_far(sides, False)
    order = (0, 1, 3, 2)
    for i, dz in enumerate(order):
        if i > 0:
            for w in (0, 1):
                to_z[dz][w].wait_recv()
            spread(dz)
            relay(order[i - 1])
        if i == 1:
            over.wait_recv()
            sides = [pass_on(strip(0, True), strip(0, True), to) for to in (right, left)]
        if i == 2:
            ends += tokens_far(sides, True)
        if i > 1:
            finish(order[i - 2])
    for copy in ends:
        copy.wait_recv()
    relay(order[Z - 1])
    finish(order[Z - 2])
    finish(order[Z - 1])
    for copy in to_core:
        copy.wait_recv()
    for copy in started:
        copy.wait_send()
    for copy in stay:
        copy.wait()


def gather_rows(tokens, keys, values, devices, leads):
    rows, width = keys.shape
    hbm = pl.BlockSpec(memory_space=pl.ANY)
    vmem = pl.BlockSpec(memory_space=pltpu.VMEM)
    gathered = jax.ShapeDtypeStruct((rows * devices, width), keys.dtype)
    return pl.pallas_call(
        gather_kernel,
        out_shape=(
            jax.ShapeDtypeStruct((rows, tokens.shape[1] * leads), tokens.dtype),
            gathered,
            gathered,
        ),
        in_specs=[hbm, hbm, hbm],
        out_specs=(vmem, hbm, hbm),
        scratch_shapes=[
            pltpu.SemaphoreType.DMA((COPIES,)),
            pltpu.SemaphoreType.DMA((COPIES,)),
            pltpu.SemaphoreType.DMA((3,)),
        ],
        compiler_params=pltpu.CompilerParams(
            collective_id=0, has_side_effects=True, vmem_limit_bytes=48 << 20
        ),
        name="gather_all",
    )(tokens, keys, values)


CHUNKS = 4


def reduce_kernel(part, out, held, relayed, outgoing, incoming, sums, send, recv):
    rows = part.shape[0] // (X * HI)
    wide = part.shape[1] // CHUNKS
    me = lax.axis_index("tp")
    x, hi = me // HI, me % HI
    right = {"tp": (x + 1) % X * HI + hi}
    left = {"tp": (x + X - 1) % X * HI + hi}
    across = {"tp": x * HI + 1 - hi}
    greet([left, right, across])

    def piece(dx, first, count, chunk):
        start = pl.multiple_of(((x + dx) % X * HI + first) * rows, rows)
        return part.at[pl.ds(start, count * rows), pl.ds(chunk * wide, wide)]

    def cols(chunk):
        return slice(chunk * wide, (chunk + 1) * wide)

    def copy(src, dst, chunk, kind, where):
        made = remote(src, dst, send.at[chunk, kind], recv.at[chunk, kind], where)
        made.start()
        return made

    copies = [[None] * 7 for _ in range(CHUNKS)]

    def begin(c):
        mine = copies[c]
        mine[2] = copy(piece(2, 0, 1, c), relayed.at[0, c], c, 2, right)
        mine[3] = copy(piece(2, 1, 1, c), relayed.at[1, c], c, 3, left)
        mine[0] = copy(piece(1, 0, 2, c), held.at[0, c], c, 0, right)
        mine[1] = copy(piece(3, 0, 2, c), held.at[1, c], c, 1, left)

    def forward(c):
        mine = copies[c]
        mine[2].wait_recv()
        mine[4] = copy(relayed.at[0, c], held.at[2, c, pl.ds(0, rows)], c, 4, right)
        mine[3].wait_recv()
        mine[5] = copy(relayed.at[1, c], held.at[2, c, pl.ds(rows, rows)], c, 5, left)

    def total(c, half):
        start = pl.multiple_of(half * rows, rows)
        own = pl.multiple_of((x * HI + half) * rows, rows)
        result = part[pl.ds(own, rows), cols(c)].astype(jnp.float32)
        for source in range(3):
            result += held[source, c, pl.ds(start, rows)].astype(jnp.float32)
        return result

    def combine(c):
        mine = copies[c]
        for kind in (0, 1, 4, 5):
            mine[kind].wait_recv()
        outgoing[c] = total(c, 1 - hi).astype(jnp.bfloat16)
        sums[c] = total(c, hi)
        mine[6] = copy(outgoing.at[c], incoming.at[c], c, 6, across)

    for c in range(CHUNKS):
        begin(c)
    for c in range(CHUNKS):
        forward(c)
        if c > 0:
            combine(c - 1)
    combine(CHUNKS - 1)
    for c in range(CHUNKS):
        copies[c][6].wait_recv()
        out[:, cols(c)] = sums[c] + incoming[c].astype(jnp.float32)
    for mine in copies:
        for made in mine:
            made.wait_send()


def reduce_rows(part):
    rows, width = part.shape[0] // (X * HI), part.shape[1]
    wide = width // CHUNKS
    vmem = pl.BlockSpec(memory_space=pltpu.VMEM)
    return pl.pallas_call(
        reduce_kernel,
        out_shape=jax.ShapeDtypeStruct((rows, width), jnp.float32),
        in_specs=[vmem],
        out_specs=vmem,
        scratch_shapes=[
            pltpu.VMEM((3, CHUNKS, HI * rows, wide), jnp.bfloat16),
            pltpu.VMEM((2, CHUNKS, rows, wide), jnp.bfloat16),
            pltpu.VMEM((CHUNKS, rows, wide), jnp.bfloat16),
            pltpu.VMEM((CHUNKS, rows, wide), jnp.bfloat16),
            pltpu.VMEM((CHUNKS, rows, wide), jnp.float32),
            pltpu.SemaphoreType.DMA((CHUNKS, 7)),
            pltpu.SemaphoreType.DMA((CHUNKS, 7)),
        ],
        compiler_params=pltpu.CompilerParams(
            collective_id=1, has_side_effects=True, vmem_limit_bytes=24 << 20
        ),
        cost_estimate=pl.CostEstimate(flops=0, bytes_accessed=100_000_000, transcendentals=0),
        name="reduce_branch",
    )(part)


def per_device(
    tokens, queries, key_rows, value_rows, clip_ids, causal, modulation, w_mlp, w_attn_out, w_mlp_out
):
    local_rows = queries.shape[0]
    tp_size = lax.axis_size("tp")
    clips = causal.shape[0]
    first_row = lax.axis_index("ctx") * local_rows
    whole_rows, key_all, value_all = gather_rows(
        tokens, key_rows, value_rows, lax.axis_size("ctx"), tp_size
    )
    numbers = jnp.arange(clips, dtype=jnp.int32)
    clip_end = jnp.sum((clip_ids[None, :] <= numbers[:, None]).astype(jnp.int32), axis=1)
    own_ids = clips_at(first_row + jnp.arange(local_rows, dtype=jnp.int32), clip_end)
    token_values = whole_rows.astype(jnp.float32)
    row_mean = jnp.mean(token_values, axis=1, keepdims=True)
    centred = token_values - row_mean
    row_var = jnp.mean(centred * centred, axis=1, keepdims=True)
    normed = centred * lax.rsqrt(row_var + eps_norm)
    shift_rows = pick_rows(own_ids, modulation[0])
    scale_rows = pick_rows(own_ids, modulation[1])
    modulated = (normed * (1.0 + scale_rows) + shift_rows).astype(jnp.bfloat16)
    hidden = jax.nn.gelu(
        jnp.dot(modulated, w_mlp, preferred_element_type=jnp.float32), approximate=True
    ).astype(jnp.bfloat16)

    attended = attention(queries, key_all, value_all, jnp.concatenate([clip_end, causal]))
    part = jnp.dot(attended, w_attn_out, preferred_element_type=jnp.float32) + jnp.dot(
        hidden, w_mlp_out, preferred_element_type=jnp.float32
    )
    branch = reduce_rows(part.astype(jnp.bfloat16))
    share_rows = local_rows // tp_size
    first_share = lax.axis_index("tp") * share_rows
    share_ids = clips_at(
        first_row + first_share + jnp.arange(share_rows, dtype=jnp.int32), clip_end
    )
    residual = lax.dynamic_slice_in_dim(whole_rows, first_share, share_rows, 0).astype(jnp.float32)
    return residual + pick_rows(share_ids, modulation[2]) * branch


def solution(mesh):
    in_specs = (
        P("ctx", "tp"), P("ctx", "tp"), P("ctx", "tp"), P("ctx", "tp"),
        P(), P(), P(), P(None, "tp"), P("tp", None), P("tp", None),
    )
    out_specs = P(("ctx", "tp"), None)
    return jax.shard_map(
        per_device, mesh=mesh, in_specs=in_specs, out_specs=out_specs, check_vma=False
    )
```

```python
import functools
import math

import jax
import jax.numpy as jnp
from jax import lax
from jax.experimental import pallas as pl
from jax.experimental.pallas import tpu as pltpu
from jax.sharding import PartitionSpec as P

HD = 128
TILE = 1024
neg_large = -1e30
eps_norm = 1e-06


def pick_rows(clip_rows, table):
    out = jnp.broadcast_to(table[0][None, :], (clip_rows.shape[0], table.shape[1]))
    for clip in range(1, table.shape[0]):
        out = jnp.where(clip_rows[:, None] == clip, table[clip][None, :], out)
    return out


def interval(table, first, rows):
    clips = table.shape[0] // 2

    def clip_of(pos):
        number = jnp.int32(0)
        for clip in range(clips - 1):
            number = number + (pos >= table[clip]).astype(jnp.int32)
        return number

    def start_of(number):
        return jnp.where(number == 0, 0, table[jnp.maximum(number - 1, 0)])

    low, high = clip_of(first), clip_of(first + rows - 1)
    end = jnp.where(table[clips + high] == 0, table[high], first + rows)
    whole_end = jnp.where(table[clips + low] == 0, table[low], first + 1)
    return start_of(low), end, start_of(high), whole_end


def clips_at(positions, clip_end):
    return jnp.sum((positions[:, None] >= clip_end[None, :-1]).astype(jnp.int32), axis=1)


def attend_kernel(table, q_ref, k_ref, v_ref, out_ref, acc, peak, edges):
    step = pl.program_id(0)
    rows = q_ref.shape[0]
    clips = table.shape[0] // 2
    first = lax.axis_index("ctx") * rows
    some_low, some_high, whole_low, whole_high = interval(table, first, rows)
    tile = some_low // TILE + step
    factor = math.log2(math.e) / math.sqrt(HD)
    heads = q_ref.shape[1] // HD

    @pl.when(step == 0)
    def _():
        acc[...] = jnp.zeros_like(acc)
        peak[...] = jnp.full_like(peak, neg_large)
        pos = first + lax.broadcasted_iota(jnp.int32, (rows, HD), 0)
        start = jnp.zeros_like(pos)
        end = jnp.where(table[clips] == 0, table[0], pos + 1)
        for clip in range(1, clips):
            later = pos >= table[clip - 1]
            start = jnp.where(later, table[clip - 1], start)
            end = jnp.where(
                later, jnp.where(table[clips + clip] == 0, table[clip], pos + 1), end
            )
        edges[0] = start
        edges[1] = end

    def one_tile(masked):
        if masked:
            pos = tile * TILE + lax.broadcasted_iota(jnp.int32, (rows, TILE), 1)
            allowed = (pos >= edges[0][:, :1]) & (pos < edges[1][:, :1])
        ones = jnp.ones((TILE, HD), jnp.bfloat16)
        for head in range(heads):
            cols = slice(head * HD, (head + 1) * HD)
            scores = lax.dot_general(
                q_ref[:, cols], k_ref[:, cols], (((1,), (1,)), ((), ())),
                preferred_element_type=jnp.float32,
            )
            if masked:
                scores = jnp.where(allowed, scores, neg_large)
            old = peak[head]
            new = jnp.maximum(old, jnp.max(scores, axis=1, keepdims=True))
            weights = jnp.exp2((scores - new[:, :1]) * factor)
            if masked:
                weights = jnp.where(allowed, weights, 0.0)
            shrink = jnp.exp2((old - new) * factor)
            values = jnp.concatenate([v_ref[:, cols], ones], axis=1)
            added = jnp.dot(
                weights.astype(jnp.bfloat16), values, preferred_element_type=jnp.float32
            )
            acc[head] = acc[head] * jnp.concatenate([shrink, shrink], axis=1) + added
            peak[head] = new

    active = tile * TILE < some_high
    whole = (tile * TILE >= whole_low) & ((tile + 1) * TILE <= whole_high)

    @pl.when(active & whole)
    def _():
        one_tile(False)

    @pl.when(active & jnp.logical_not(whole))
    def _():
        one_tile(True)

    @pl.when(step == pl.num_programs(0) - 1)
    def _():
        for head in range(heads):
            out_ref[:, head * HD:(head + 1) * HD] = (
                acc[head][:, :HD] / acc[head][:, HD:]
            ).astype(out_ref.dtype)


def attention(queries, keys, values, table):
    rows, width = queries.shape
    tiles = keys.shape[0] // TILE

    def kv_map(step, table):
        low, high, _, _ = interval(table, lax.axis_index("ctx") * rows, rows)
        return (jnp.minimum(low // TILE + step, (high - 1) // TILE), 0)

    def fixed(step, table):
        return (0, 0)

    return pl.pallas_call(
        attend_kernel,
        out_shape=jax.ShapeDtypeStruct((rows, width), jnp.bfloat16),
        grid_spec=pltpu.PrefetchScalarGridSpec(
            num_scalar_prefetch=1,
            grid=(tiles,),
            in_specs=[
                pl.BlockSpec((rows, width), fixed),
                pl.BlockSpec((TILE, width), kv_map),
                pl.BlockSpec((TILE, width), kv_map),
            ],
            out_specs=pl.BlockSpec((rows, width), fixed),
            scratch_shapes=[
                pltpu.VMEM((width // HD, rows, 2 * HD), jnp.float32),
                pltpu.VMEM((width // HD, rows, HD), jnp.float32),
                pltpu.VMEM((2, rows, HD), jnp.int32),
            ],
        ),
        compiler_params=pltpu.CompilerParams(vmem_limit_bytes=60 << 20),
        cost_estimate=pl.CostEstimate(
            flops=8 * rows * keys.shape[0] * width,
            bytes_accessed=4 * keys.shape[0] * width,
            transcendentals=rows * keys.shape[0] * width // HD,
        ),
        name="attend",
    )(table, queries, keys, values)


def remote(src, dst, send_sem, recv_sem, where):
    return pltpu.make_async_remote_copy(
        src_ref=src, dst_ref=dst, send_sem=send_sem, recv_sem=recv_sem,
        device_id=where, device_id_type=pl.DeviceIdType.MESH,
    )


def greet(places):
    barrier = pltpu.get_barrier_semaphore()
    for place in places:
        pl.semaphore_signal(
            barrier, inc=1, device_id=place, device_id_type=pl.DeviceIdType.MESH
        )
    pl.semaphore_wait(barrier, len(places))


Y, Z, CORES = 4, 4, 2
X, HI = 4, 2
COPIES = 2 * (Z - 1) + 6 * Z + 2 * Y * Z + 9


LN_ROWS = 32


def gather_kernel(
    ends_ref, modulation, tokens, keys, values, w_in_hbm, w_out_hbm,
    whole, key_all, value_all, part,
    w_in, w_out, modulated, hidden, send, recv, local,
):
    rows = keys.shape[0]
    me = lax.axis_index("ctx")
    y, z, core = me // (Z * CORES), me // CORES % Z, me % CORES
    pair = (key_all, value_all)
    own = (keys, values)

    def index(dy, dz, flip=False):
        other = 1 - core if flip else core
        return ((y + dy + Y) % Y * Z + (z + dz + Z) % Z) * CORES + other

    def slot(which, dy, dz, flip=False):
        start = pl.multiple_of(index(dy, dz, flip) * rows, rows)
        return pair[which].at[pl.ds(start, rows)]

    def at(dy, dz, flip=False):
        return {"ctx": index(dy, dz, flip)}

    lead = lax.axis_index("tp")
    x, hi = lead // HI, lead % HI
    half, wide = tokens.shape[0] // 2, tokens.shape[1]

    def column(dx, flip=False):
        return (x + dx + X) % X * HI + (1 - hi if flip else hi)

    def strip(dx, flip=False, part=None):
        cols = pl.ds(pl.multiple_of(column(dx, flip) * wide, wide), wide)
        if part is None:
            return whole.at[:, cols]
        return whole.at[pl.ds(part * half, half), cols]

    right, left = {"tp": column(1)}, {"tp": column(-1)}
    across = {"tp": column(0, True)}
    greet(
        [at(0, d) for d in range(1, Z)]
        + [at(1, 0), at(-1, 0), at(0, 0, True), right, left, across]
    )
    started = []
    made = [0]

    def pass_on(src, dst, where):
        number = made[0]
        made[0] += 1
        copy = remote(src, dst, send.at[number], recv.at[number], where)
        copy.start()
        started.append(copy)
        return copy

    over = pass_on(tokens, strip(0), across)
    sides = [pass_on(tokens, strip(0), right), pass_on(tokens, strip(0), left)]

    def make(src, which, owner, target):
        return pass_on(src, slot(which, *owner), at(*target))

    stay = [pltpu.make_async_copy(own[w], slot(w, 0, 0), local.at[w]) for w in (0, 1)]
    stay.append(pltpu.make_async_copy(tokens, strip(0), local.at[2]))
    weights = [
        pltpu.make_async_copy(w_in_hbm, w_in, local.at[3]),
        pltpu.make_async_copy(w_out_hbm, w_out, local.at[4]),
    ]
    stay += weights
    for copy in stay:
        copy.start()
    near = [[None] * 4 for _ in range(Z)]
    far = [[None] * 2 for _ in range(Z)]
    to_z = [[None] * 2 for _ in range(Z)]
    to_core = []

    def spread(dz):
        for w in (0, 1):
            src = own[w] if dz == 0 else slot(w, 0, dz)
            near[dz][w] = make(src, w, (0, dz), (1, 0))
            near[dz][2 + w] = make(src, w, (0, dz), (-1, 0))
            to_core.append(make(src, w, (0, dz), (0, 0, True)))

    def relay(dz):
        near[dz][0].wait_recv()
        far[dz][0] = make(slot(0, -1, dz), 0, (-1, dz), (1, 0))
        near[dz][3].wait_recv()
        far[dz][1] = make(slot(1, 1, dz), 1, (1, dz), (-1, 0))
        near[dz][1].wait_recv()
        near[dz][2].wait_recv()
        for w in (0, 1):
            for dy in (-1, 1):
                to_core.append(make(slot(w, dy, dz), w, (dy, dz), (0, 0, True)))

    def finish(dz):
        for w in (0, 1):
            far[dz][w].wait_recv()
            to_core.append(make(slot(w, 2, dz), w, (2, dz), (0, 0, True)))

    for d in (1, 3, 2):
        for w in (0, 1):
            to_z[Z - d][w] = make(own[w], w, (0, 0), (0, d))
    spread(0)

    def tokens_far(arrived, flip):
        for copy in arrived:
            copy.wait_recv()
        return [
            pass_on(strip(-1, flip, 0), strip(-1, flip, 0), right),
            pass_on(strip(1, flip, 1), strip(1, flip, 1), left),
        ]

    def normalize(first, last):
        @pl.loop(first // LN_ROWS, last // LN_ROWS)
        def _(block):
            start = pl.multiple_of(block * LN_ROWS, LN_ROWS)
            values = whole[pl.ds(start, LN_ROWS), :].astype(jnp.float32)
            centred = values - jnp.mean(values, axis=1, keepdims=True)
            variance = jnp.mean(centred * centred, axis=1, keepdims=True)
            normed = centred * lax.rsqrt(variance + eps_norm)
            pos = me * rows + start + lax.broadcasted_iota(jnp.int32, (LN_ROWS, 1), 0)
            shift = jnp.broadcast_to(modulation[0, 0:1, :], normed.shape)
            scale = jnp.broadcast_to(modulation[1, 0:1, :], normed.shape)
            for clip in range(1, modulation.shape[1]):
                later = pos >= ends_ref[clip - 1]
                shift = jnp.where(later, modulation[0, clip:clip + 1, :], shift)
                scale = jnp.where(later, modulation[1, clip:clip + 1, :], scale)
            modulated[pl.ds(start, LN_ROWS), :] = (normed * (1.0 + scale) + shift).astype(
                modulated.dtype
            )

    def project(source, weight, target, width, finish_tile):
        @pl.loop(0, weight.shape[1] // width)
        def _(block):
            cols = pl.ds(pl.multiple_of(block * width, width), width)
            target[:, cols] = finish_tile(
                jnp.dot(source[...], weight[:, cols], preferred_element_type=jnp.float32)
            ).astype(target.dtype)

    ends = tokens_far(sides, False)
    order = (0, 1, 3, 2)
    for i, dz in enumerate(order):
        if i > 0:
            for w in (0, 1):
                to_z[dz][w].wait_recv()
            spread(dz)
            if i == 3:
                normalize(rows // 2, rows)
            relay(order[i - 1])
        if i == 1:
            over.wait_recv()
            sides = [pass_on(strip(0, True), strip(0, True), to) for to in (right, left)]
        if i == 2:
            ends += tokens_far(sides, True)
        if i > 1:
            finish(order[i - 2])
        if i == 2:
            for copy in ends:
                copy.wait_recv()
            for copy in stay:
                copy.wait()
            normalize(0, rows // 2)
    project(
        modulated, w_in, hidden, 256, functools.partial(jax.nn.gelu, approximate=True)
    )
    relay(order[Z - 1])
    project(hidden, w_out, part, 512, lambda tile: tile)
    finish(order[Z - 2])
    finish(order[Z - 1])
    for copy in to_core:
        copy.wait_recv()
    for copy in started:
        copy.wait_send()


def gather_rows(clip_end, modulation, tokens, keys, values, w_in, w_out, devices, leads):
    rows, width = keys.shape
    hbm = pl.BlockSpec(memory_space=pl.ANY)
    vmem = pl.BlockSpec(memory_space=pltpu.VMEM)
    gathered = jax.ShapeDtypeStruct((rows * devices, width), keys.dtype)
    return pl.pallas_call(
        gather_kernel,
        out_shape=(
            jax.ShapeDtypeStruct((rows, tokens.shape[1] * leads), tokens.dtype),
            gathered,
            gathered,
            jax.ShapeDtypeStruct((rows, w_out.shape[1]), jnp.float32),
        ),
        in_specs=[pl.BlockSpec(memory_space=pltpu.SMEM), vmem, hbm, hbm, hbm, hbm, hbm],
        out_specs=(vmem, hbm, hbm, vmem),
        scratch_shapes=[
            pltpu.VMEM(w_in.shape, w_in.dtype),
            pltpu.VMEM(w_out.shape, w_out.dtype),
            pltpu.VMEM((rows, w_in.shape[0]), jnp.bfloat16),
            pltpu.VMEM((rows, w_in.shape[1]), jnp.bfloat16),
            pltpu.SemaphoreType.DMA((COPIES,)),
            pltpu.SemaphoreType.DMA((COPIES,)),
            pltpu.SemaphoreType.DMA((5,)),
        ],
        compiler_params=pltpu.CompilerParams(
            collective_id=0, has_side_effects=True, vmem_limit_bytes=60 << 20
        ),
        name="gather_all",
    )(clip_end, modulation, tokens, keys, values, w_in, w_out)


CHUNKS = 4


def reduce_kernel(part, out, held, relayed, outgoing, incoming, sums, send, recv):
    rows = part.shape[0] // (X * HI)
    wide = part.shape[1] // CHUNKS
    me = lax.axis_index("tp")
    x, hi = me // HI, me % HI
    right = {"tp": (x + 1) % X * HI + hi}
    left = {"tp": (x + X - 1) % X * HI + hi}
    across = {"tp": x * HI + 1 - hi}
    greet([left, right, across])

    def piece(dx, first, count, chunk):
        start = pl.multiple_of(((x + dx) % X * HI + first) * rows, rows)
        return part.at[pl.ds(start, count * rows), pl.ds(chunk * wide, wide)]

    def cols(chunk):
        return slice(chunk * wide, (chunk + 1) * wide)

    def copy(src, dst, chunk, kind, where):
        made = remote(src, dst, send.at[chunk, kind], recv.at[chunk, kind], where)
        made.start()
        return made

    copies = [[None] * 7 for _ in range(CHUNKS)]

    def begin(c):
        mine = copies[c]
        mine[2] = copy(piece(2, 0, 1, c), relayed.at[0, c], c, 2, right)
        mine[3] = copy(piece(2, 1, 1, c), relayed.at[1, c], c, 3, left)
        mine[0] = copy(piece(1, 0, 2, c), held.at[0, c], c, 0, right)
        mine[1] = copy(piece(3, 0, 2, c), held.at[1, c], c, 1, left)

    def forward(c):
        mine = copies[c]
        mine[2].wait_recv()
        mine[4] = copy(relayed.at[0, c], held.at[2, c, pl.ds(0, rows)], c, 4, right)
        mine[3].wait_recv()
        mine[5] = copy(relayed.at[1, c], held.at[2, c, pl.ds(rows, rows)], c, 5, left)

    def total(c, half):
        start = pl.multiple_of(half * rows, rows)
        own = pl.multiple_of((x * HI + half) * rows, rows)
        result = part[pl.ds(own, rows), cols(c)].astype(jnp.float32)
        for source in range(3):
            result += held[source, c, pl.ds(start, rows)].astype(jnp.float32)
        return result

    def combine(c):
        mine = copies[c]
        for kind in (0, 1, 4, 5):
            mine[kind].wait_recv()
        outgoing[c] = total(c, 1 - hi).astype(jnp.bfloat16)
        sums[c] = total(c, hi)
        mine[6] = copy(outgoing.at[c], incoming.at[c], c, 6, across)

    for c in range(CHUNKS):
        begin(c)
    for c in range(CHUNKS):
        forward(c)
        if c > 0:
            combine(c - 1)
    combine(CHUNKS - 1)
    for c in range(CHUNKS):
        copies[c][6].wait_recv()
        out[:, cols(c)] = sums[c] + incoming[c].astype(jnp.float32)
    for mine in copies:
        for made in mine:
            made.wait_send()


def reduce_rows(part):
    rows, width = part.shape[0] // (X * HI), part.shape[1]
    wide = width // CHUNKS
    vmem = pl.BlockSpec(memory_space=pltpu.VMEM)
    return pl.pallas_call(
        reduce_kernel,
        out_shape=jax.ShapeDtypeStruct((rows, width), jnp.float32),
        in_specs=[vmem],
        out_specs=vmem,
        scratch_shapes=[
            pltpu.VMEM((3, CHUNKS, HI * rows, wide), jnp.bfloat16),
            pltpu.VMEM((2, CHUNKS, rows, wide), jnp.bfloat16),
            pltpu.VMEM((CHUNKS, rows, wide), jnp.bfloat16),
            pltpu.VMEM((CHUNKS, rows, wide), jnp.bfloat16),
            pltpu.VMEM((CHUNKS, rows, wide), jnp.float32),
            pltpu.SemaphoreType.DMA((CHUNKS, 7)),
            pltpu.SemaphoreType.DMA((CHUNKS, 7)),
        ],
        compiler_params=pltpu.CompilerParams(
            collective_id=1, has_side_effects=True, vmem_limit_bytes=24 << 20
        ),
        cost_estimate=pl.CostEstimate(flops=0, bytes_accessed=100_000_000, transcendentals=0),
        name="reduce_branch",
    )(part)


def per_device(
    tokens, queries, key_rows, value_rows, clip_ids, causal, modulation, w_mlp, w_attn_out, w_mlp_out
):
    local_rows = queries.shape[0]
    tp_size = lax.axis_size("tp")
    clips = causal.shape[0]
    first_row = lax.axis_index("ctx") * local_rows
    numbers = jnp.arange(clips, dtype=jnp.int32)
    clip_end = jnp.sum((clip_ids[None, :] <= numbers[:, None]).astype(jnp.int32), axis=1)
    whole_rows, key_all, value_all, mlp_part = gather_rows(
        clip_end, modulation, tokens, key_rows, value_rows, w_mlp, w_mlp_out,
        lax.axis_size("ctx"), tp_size,
    )
    attended = attention(queries, key_all, value_all, jnp.concatenate([clip_end, causal]))
    part = jnp.dot(attended, w_attn_out, preferred_element_type=jnp.float32) + mlp_part
    branch = reduce_rows(part.astype(jnp.bfloat16))
    share_rows = local_rows // tp_size
    first_share = lax.axis_index("tp") * share_rows
    share_ids = clips_at(
        first_row + first_share + jnp.arange(share_rows, dtype=jnp.int32), clip_end
    )
    residual = lax.dynamic_slice_in_dim(whole_rows, first_share, share_rows, 0).astype(jnp.float32)
    return residual + pick_rows(share_ids, modulation[2]) * branch


def solution(mesh):
    in_specs = (
        P("ctx", "tp"), P("ctx", "tp"), P("ctx", "tp"), P("ctx", "tp"),
        P(), P(), P(), P(None, "tp"), P("tp", None), P("tp", None),
    )
    out_specs = P(("ctx", "tp"), None)
    return jax.shard_map(
        per_device, mesh=mesh, in_specs=in_specs, out_specs=out_specs, check_vma=False
    )
```

```python
import functools
import math

import jax
import jax.numpy as jnp
from jax import lax
from jax.experimental import pallas as pl
from jax.experimental.pallas import tpu as pltpu
from jax.sharding import PartitionSpec as P

HD = 128
TILE = 1024
neg_large = -1e30
eps_norm = 1e-06


def interval(table, first, rows):
    clips = table.shape[0] // 2

    def clip_of(pos):
        number = jnp.int32(0)
        for clip in range(clips - 1):
            number = number + (pos >= table[clip]).astype(jnp.int32)
        return number

    def start_of(number):
        return jnp.where(number == 0, 0, table[jnp.maximum(number - 1, 0)])

    low, high = clip_of(first), clip_of(first + rows - 1)
    end = jnp.where(table[clips + high] == 0, table[high], first + rows)
    whole_end = jnp.where(table[clips + low] == 0, table[low], first + 1)
    return start_of(low), end, start_of(high), whole_end


def attend_kernel(table, q_ref, k_ref, v_ref, out_ref, acc, peak, edges):
    step = pl.program_id(0)
    rows = q_ref.shape[0]
    clips = table.shape[0] // 2
    first = lax.axis_index("ctx") * rows
    some_low, some_high, whole_low, whole_high = interval(table, first, rows)
    tile = some_low // TILE + step
    factor = math.log2(math.e) / math.sqrt(HD)
    heads = q_ref.shape[1] // HD

    @pl.when(step == 0)
    def _():
        acc[...] = jnp.zeros_like(acc)
        peak[...] = jnp.full_like(peak, neg_large)
        pos = first + lax.broadcasted_iota(jnp.int32, (rows, HD), 0)
        start = jnp.zeros_like(pos)
        end = jnp.where(table[clips] == 0, table[0], pos + 1)
        for clip in range(1, clips):
            later = pos >= table[clip - 1]
            start = jnp.where(later, table[clip - 1], start)
            end = jnp.where(
                later, jnp.where(table[clips + clip] == 0, table[clip], pos + 1), end
            )
        edges[0] = start
        edges[1] = end

    def one_tile(masked):
        if masked:
            pos = tile * TILE + lax.broadcasted_iota(jnp.int32, (rows, TILE), 1)
            allowed = (pos >= edges[0][:, :1]) & (pos < edges[1][:, :1])
        ones = jnp.ones((TILE, HD), jnp.bfloat16)
        for head in range(heads):
            cols = slice(head * HD, (head + 1) * HD)
            scores = lax.dot_general(
                q_ref[:, cols], k_ref[:, cols], (((1,), (1,)), ((), ())),
                preferred_element_type=jnp.float32,
            )
            if masked:
                scores = jnp.where(allowed, scores, neg_large)
            old = peak[head]
            new = jnp.maximum(old, jnp.max(scores, axis=1, keepdims=True))
            weights = jnp.exp2((scores - new[:, :1]) * factor)
            if masked:
                weights = jnp.where(allowed, weights, 0.0)
            shrink = jnp.exp2((old - new) * factor)
            values = jnp.concatenate([v_ref[:, cols], ones], axis=1)
            added = jnp.dot(
                weights.astype(jnp.bfloat16), values, preferred_element_type=jnp.float32
            )
            acc[head] = acc[head] * jnp.concatenate([shrink, shrink], axis=1) + added
            peak[head] = new

    active = tile * TILE < some_high
    whole = (tile * TILE >= whole_low) & ((tile + 1) * TILE <= whole_high)

    @pl.when(active & whole)
    def _():
        one_tile(False)

    @pl.when(active & jnp.logical_not(whole))
    def _():
        one_tile(True)

    @pl.when(step == pl.num_programs(0) - 1)
    def _():
        for head in range(heads):
            out_ref[:, head * HD:(head + 1) * HD] = (
                acc[head][:, :HD] / acc[head][:, HD:]
            ).astype(out_ref.dtype)


def attention(queries, keys, values, table):
    rows, width = queries.shape
    tiles = keys.shape[0] // TILE

    def kv_map(step, table):
        low, high, _, _ = interval(table, lax.axis_index("ctx") * rows, rows)
        return (jnp.minimum(low // TILE + step, (high - 1) // TILE), 0)

    def fixed(step, table):
        return (0, 0)

    return pl.pallas_call(
        attend_kernel,
        out_shape=jax.ShapeDtypeStruct((rows, width), jnp.bfloat16),
        grid_spec=pltpu.PrefetchScalarGridSpec(
            num_scalar_prefetch=1,
            grid=(tiles,),
            in_specs=[
                pl.BlockSpec((rows, width), fixed),
                pl.BlockSpec((TILE, width), kv_map),
                pl.BlockSpec((TILE, width), kv_map),
            ],
            out_specs=pl.BlockSpec((rows, width), fixed),
            scratch_shapes=[
                pltpu.VMEM((width // HD, rows, 2 * HD), jnp.float32),
                pltpu.VMEM((width // HD, rows, HD), jnp.float32),
                pltpu.VMEM((2, rows, HD), jnp.int32),
            ],
        ),
        compiler_params=pltpu.CompilerParams(vmem_limit_bytes=60 << 20),
        cost_estimate=pl.CostEstimate(
            flops=8 * rows * keys.shape[0] * width,
            bytes_accessed=4 * keys.shape[0] * width,
            transcendentals=rows * keys.shape[0] * width // HD,
        ),
        name="attend",
    )(table, queries, keys, values)


def remote(src, dst, send_sem, recv_sem, where):
    return pltpu.make_async_remote_copy(
        src_ref=src, dst_ref=dst, send_sem=send_sem, recv_sem=recv_sem,
        device_id=where, device_id_type=pl.DeviceIdType.MESH,
    )


def greet(places):
    barrier = pltpu.get_barrier_semaphore()
    for place in places:
        pl.semaphore_signal(
            barrier, inc=1, device_id=place, device_id_type=pl.DeviceIdType.MESH
        )
    pl.semaphore_wait(barrier, len(places))


Y, Z, CORES = 4, 4, 2
X, HI = 4, 2
COPIES = 2 * (Z - 1) + 6 * Z + 2 * Y * Z + 12


LN_ROWS = 32


def gather_kernel(
    ends_ref, modulation, tokens, keys, values, w_in_hbm, w_out_hbm,
    whole, key_all, value_all, part,
    w_in, w_out, modulated, hidden, halfway, send, recv, local,
):
    rows = keys.shape[0]
    me = lax.axis_index("ctx")
    y, z, core = me // (Z * CORES), me // CORES % Z, me % CORES
    pair = (key_all, value_all)
    own = (keys, values)

    def index(dy, dz, flip=False):
        other = 1 - core if flip else core
        return ((y + dy + Y) % Y * Z + (z + dz + Z) % Z) * CORES + other

    def slot(which, dy, dz, flip=False):
        start = pl.multiple_of(index(dy, dz, flip) * rows, rows)
        return pair[which].at[pl.ds(start, rows)]

    def at(dy, dz, flip=False):
        return {"ctx": index(dy, dz, flip)}

    lead = lax.axis_index("tp")
    x, hi = lead // HI, lead % HI
    half, wide = tokens.shape[0] // 2, tokens.shape[1]

    def column(dx, flip=False):
        return (x + dx + X) % X * HI + (1 - hi if flip else hi)

    def strip(dx, flip=False, part=None):
        cols = pl.ds(pl.multiple_of(column(dx, flip) * wide, wide), wide)
        if part is None:
            return whole.at[:, cols]
        return whole.at[pl.ds(part * half, half), cols]

    right, left = {"tp": column(1)}, {"tp": column(-1)}
    depth = hi * Z + z

    def along(steps):
        place = (depth + steps + Z * HI) % (Z * HI)
        return {"ctx": (y * Z + place % Z) * CORES + core, "tp": x * HI + place // Z}

    up, down = along(2), along(-2)
    greet(
        [at(0, d) for d in range(1, Z)]
        + [at(1, 0), at(-1, 0), at(0, 0, True), right, left, up, down]
    )

    def origin(steps, part):
        lead_there = along(steps)["tp"]
        cols = pl.ds(pl.multiple_of(lead_there * wide, wide), wide)
        return whole.at[pl.ds(part * half, half), cols]
    started = []
    made = [0]

    def pass_on(src, dst, where):
        number = made[0]
        made[0] += 1
        copy = remote(src, dst, send.at[number], recv.at[number], where)
        copy.start()
        started.append(copy)
        return copy

    over = [
        pass_on(tokens.at[pl.ds(0, half)], halfway.at[0], up),
        pass_on(tokens.at[pl.ds(half, half)], halfway.at[1], down),
    ]
    sides = [pass_on(tokens, strip(0), right), pass_on(tokens, strip(0), left)]

    def make(src, which, owner, target):
        return pass_on(src, slot(which, *owner), at(*target))

    stay = [pltpu.make_async_copy(own[w], slot(w, 0, 0), local.at[w]) for w in (0, 1)]
    stay.append(pltpu.make_async_copy(tokens, strip(0), local.at[2]))
    weights = [
        pltpu.make_async_copy(w_in_hbm, w_in, local.at[3]),
        pltpu.make_async_copy(w_out_hbm, w_out, local.at[4]),
    ]
    stay += weights
    for copy in stay:
        copy.start()
    near = [[None] * 4 for _ in range(Z)]
    far = [[None] * 2 for _ in range(Z)]
    to_z = [[None] * 2 for _ in range(Z)]
    to_core = []

    def spread(dz):
        for w in (0, 1):
            src = own[w] if dz == 0 else slot(w, 0, dz)
            near[dz][w] = make(src, w, (0, dz), (1, 0))
            near[dz][2 + w] = make(src, w, (0, dz), (-1, 0))
            to_core.append(make(src, w, (0, dz), (0, 0, True)))

    def relay(dz):
        near[dz][0].wait_recv()
        far[dz][0] = make(slot(0, -1, dz), 0, (-1, dz), (1, 0))
        near[dz][3].wait_recv()
        far[dz][1] = make(slot(1, 1, dz), 1, (1, dz), (-1, 0))
        near[dz][1].wait_recv()
        near[dz][2].wait_recv()
        for w in (0, 1):
            for dy in (-1, 1):
                to_core.append(make(slot(w, dy, dz), w, (dy, dz), (0, 0, True)))

    def finish(dz):
        for w in (0, 1):
            far[dz][w].wait_recv()
            to_core.append(make(slot(w, 2, dz), w, (2, dz), (0, 0, True)))

    for d in (1, 3, 2):
        for w in (0, 1):
            to_z[Z - d][w] = make(own[w], w, (0, 0), (0, d))
    spread(0)

    def tokens_far(arrived, flip):
        for copy in arrived:
            copy.wait_recv()
        return [
            pass_on(strip(-1, flip, 0), strip(-1, flip, 0), right),
            pass_on(strip(1, flip, 1), strip(1, flip, 1), left),
        ]

    def normalize(first, last):
        @pl.loop(first // LN_ROWS, last // LN_ROWS)
        def _(block):
            start = pl.multiple_of(block * LN_ROWS, LN_ROWS)
            values = whole[pl.ds(start, LN_ROWS), :].astype(jnp.float32)
            centred = values - jnp.mean(values, axis=1, keepdims=True)
            variance = jnp.mean(centred * centred, axis=1, keepdims=True)
            normed = centred * lax.rsqrt(variance + eps_norm)
            pos = me * rows + start + lax.broadcasted_iota(jnp.int32, (LN_ROWS, 1), 0)
            shift = jnp.broadcast_to(modulation[0, 0:1, :], normed.shape)
            scale = jnp.broadcast_to(modulation[1, 0:1, :], normed.shape)
            for clip in range(1, modulation.shape[1]):
                later = pos >= ends_ref[clip - 1]
                shift = jnp.where(later, modulation[0, clip:clip + 1, :], shift)
                scale = jnp.where(later, modulation[1, clip:clip + 1, :], scale)
            modulated[pl.ds(start, LN_ROWS), :] = (normed * (1.0 + scale) + shift).astype(
                modulated.dtype
            )

    def project(source, weight, target, width, finish_tile):
        @pl.loop(0, weight.shape[1] // width)
        def _(block):
            cols = pl.ds(pl.multiple_of(block * width, width), width)
            target[:, cols] = finish_tile(
                jnp.dot(source[...], weight[:, cols], preferred_element_type=jnp.float32)
            ).astype(target.dtype)

    ends = tokens_far(sides, False)
    for copy in over:
        copy.wait_recv()
    over = [
        pass_on(halfway.at[0], origin(-2, 0), up),
        pass_on(halfway.at[1], origin(2, 1), down),
    ]
    order = (0, 1, 3, 2)
    for i, dz in enumerate(order):
        if i > 0:
            for w in (0, 1):
                to_z[dz][w].wait_recv()
            spread(dz)
            if i == 3:
                normalize(rows // 2, rows)
            relay(order[i - 1])
        if i == 1:
            for copy in over:
                copy.wait_recv()
            sides = [pass_on(strip(0, True), strip(0, True), to) for to in (right, left)]
        if i == 2:
            ends += tokens_far(sides, True)
        if i > 1:
            finish(order[i - 2])
        if i == 2:
            for copy in ends:
                copy.wait_recv()
            for copy in stay:
                copy.wait()
            normalize(0, rows // 2)
    project(
        modulated, w_in, hidden, 256, functools.partial(jax.nn.gelu, approximate=True)
    )
    relay(order[Z - 1])
    project(hidden, w_out, part, 512, lambda tile: tile)
    finish(order[Z - 2])
    finish(order[Z - 1])
    for copy in to_core:
        copy.wait_recv()
    for copy in started:
        copy.wait_send()


def gather_rows(clip_end, modulation, tokens, keys, values, w_in, w_out, devices, leads):
    rows, width = keys.shape
    hbm = pl.BlockSpec(memory_space=pl.ANY)
    vmem = pl.BlockSpec(memory_space=pltpu.VMEM)
    gathered = jax.ShapeDtypeStruct((rows * devices, width), keys.dtype)
    return pl.pallas_call(
        gather_kernel,
        out_shape=(
            jax.ShapeDtypeStruct((rows, tokens.shape[1] * leads), tokens.dtype),
            gathered,
            gathered,
            jax.ShapeDtypeStruct((rows, w_out.shape[1]), jnp.float32),
        ),
        in_specs=[pl.BlockSpec(memory_space=pltpu.SMEM), vmem, hbm, hbm, hbm, hbm, hbm],
        out_specs=(vmem, hbm, hbm, vmem),
        scratch_shapes=[
            pltpu.VMEM(w_in.shape, w_in.dtype),
            pltpu.VMEM(w_out.shape, w_out.dtype),
            pltpu.VMEM((rows, w_in.shape[0]), jnp.bfloat16),
            pltpu.VMEM((rows, w_in.shape[1]), jnp.bfloat16),
            pltpu.VMEM((2, rows // 2, tokens.shape[1]), tokens.dtype),
            pltpu.SemaphoreType.DMA((COPIES,)),
            pltpu.SemaphoreType.DMA((COPIES,)),
            pltpu.SemaphoreType.DMA((5,)),
        ],
        compiler_params=pltpu.CompilerParams(
            collective_id=0, has_side_effects=True, vmem_limit_bytes=60 << 20
        ),
        name="gather_all",
    )(clip_end, modulation, tokens, keys, values, w_in, w_out)


CHUNKS = 4


def reduce_kernel(
    ends_ref, modulation, whole, part,
    out, held, relayed, outgoing, incoming, sums, residual, send, recv, local,
):
    rows = part.shape[0] // (X * HI)
    wide = part.shape[1] // CHUNKS
    me = lax.axis_index("tp")
    x, hi = me // HI, me % HI
    right = {"tp": (x + 1) % X * HI + hi}
    left = {"tp": (x + X - 1) % X * HI + hi}
    across = {"tp": x * HI + 1 - hi}
    greet([left, right, across])
    mine = pl.ds(pl.multiple_of(me * rows, rows), rows)
    fetch = pltpu.make_async_copy(whole.at[mine], residual, local)
    fetch.start()

    def piece(dx, first, count, chunk):
        start = pl.multiple_of(((x + dx) % X * HI + first) * rows, rows)
        return part.at[pl.ds(start, count * rows), pl.ds(chunk * wide, wide)]

    def cols(chunk):
        return slice(chunk * wide, (chunk + 1) * wide)

    def copy(src, dst, chunk, kind, where):
        made = remote(src, dst, send.at[chunk, kind], recv.at[chunk, kind], where)
        made.start()
        return made

    copies = [[None] * 7 for _ in range(CHUNKS)]

    def begin(c):
        mine = copies[c]
        mine[2] = copy(piece(2, 0, 1, c), relayed.at[0, c], c, 2, right)
        mine[3] = copy(piece(2, 1, 1, c), relayed.at[1, c], c, 3, left)
        mine[0] = copy(piece(1, 0, 2, c), held.at[0, c], c, 0, right)
        mine[1] = copy(piece(3, 0, 2, c), held.at[1, c], c, 1, left)

    def forward(c):
        mine = copies[c]
        mine[2].wait_recv()
        mine[4] = copy(relayed.at[0, c], held.at[2, c, pl.ds(0, rows)], c, 4, right)
        mine[3].wait_recv()
        mine[5] = copy(relayed.at[1, c], held.at[2, c, pl.ds(rows, rows)], c, 5, left)

    def total(c, half):
        start = pl.multiple_of(half * rows, rows)
        own = pl.multiple_of((x * HI + half) * rows, rows)
        result = part[pl.ds(own, rows), cols(c)].astype(jnp.float32)
        for source in range(3):
            result += held[source, c, pl.ds(start, rows)].astype(jnp.float32)
        return result

    def combine(c):
        mine = copies[c]
        for kind in (0, 1, 4, 5):
            mine[kind].wait_recv()
        outgoing[c] = total(c, 1 - hi).astype(jnp.bfloat16)
        sums[c] = total(c, hi)
        mine[6] = copy(outgoing.at[c], incoming.at[c], c, 6, across)

    for c in range(CHUNKS):
        begin(c)
    for c in range(CHUNKS):
        forward(c)
        if c > 0:
            combine(c - 1)
    combine(CHUNKS - 1)
    fetch.wait()
    first = (lax.axis_index("ctx") * X * HI + me) * rows
    pos = first + lax.broadcasted_iota(jnp.int32, (rows, 1), 0)
    for c in range(CHUNKS):
        copies[c][6].wait_recv()
        branch = sums[c] + incoming[c].astype(jnp.float32)
        gate = jnp.broadcast_to(modulation[2, 0:1, cols(c)], branch.shape)
        for clip in range(1, modulation.shape[1]):
            later = pos >= ends_ref[clip - 1]
            gate = jnp.where(later, modulation[2, clip:clip + 1, cols(c)], gate)
        out[:, cols(c)] = residual[:, cols(c)].astype(jnp.float32) + gate * branch
    for mine in copies:
        for made in mine:
            made.wait_send()


def reduce_rows(clip_end, modulation, whole, part):
    rows, width = part.shape[0] // (X * HI), part.shape[1]
    wide = width // CHUNKS
    vmem = pl.BlockSpec(memory_space=pltpu.VMEM)
    return pl.pallas_call(
        reduce_kernel,
        out_shape=jax.ShapeDtypeStruct((rows, width), jnp.float32),
        in_specs=[
            pl.BlockSpec(memory_space=pltpu.SMEM), vmem, pl.BlockSpec(memory_space=pl.ANY), vmem
        ],
        out_specs=vmem,
        scratch_shapes=[
            pltpu.VMEM((3, CHUNKS, HI * rows, wide), jnp.bfloat16),
            pltpu.VMEM((2, CHUNKS, rows, wide), jnp.bfloat16),
            pltpu.VMEM((CHUNKS, rows, wide), jnp.bfloat16),
            pltpu.VMEM((CHUNKS, rows, wide), jnp.bfloat16),
            pltpu.VMEM((CHUNKS, rows, wide), jnp.float32),
            pltpu.VMEM((rows, width), jnp.bfloat16),
            pltpu.SemaphoreType.DMA((CHUNKS, 7)),
            pltpu.SemaphoreType.DMA((CHUNKS, 7)),
            pltpu.SemaphoreType.DMA,
        ],
        compiler_params=pltpu.CompilerParams(
            collective_id=1, has_side_effects=True, vmem_limit_bytes=24 << 20
        ),
        cost_estimate=pl.CostEstimate(flops=0, bytes_accessed=100_000_000, transcendentals=0),
        name="reduce_branch",
    )(clip_end, modulation, whole, part)


def per_device(
    tokens, queries, key_rows, value_rows, clip_ids, causal, modulation, w_mlp, w_attn_out, w_mlp_out
):
    local_rows = queries.shape[0]
    tp_size = lax.axis_size("tp")
    clips = causal.shape[0]
    numbers = jnp.arange(clips, dtype=jnp.int32)
    clip_end = jnp.sum((clip_ids[None, :] <= numbers[:, None]).astype(jnp.int32), axis=1)
    whole_rows, key_all, value_all, mlp_part = gather_rows(
        clip_end, modulation, tokens, key_rows, value_rows, w_mlp, w_mlp_out,
        lax.axis_size("ctx"), tp_size,
    )
    attended = attention(queries, key_all, value_all, jnp.concatenate([clip_end, causal]))
    part = jnp.dot(attended, w_attn_out, preferred_element_type=jnp.float32) + mlp_part
    return reduce_rows(clip_end, modulation, whole_rows, part.astype(jnp.bfloat16))


def solution(mesh):
    in_specs = (
        P("ctx", "tp"), P("ctx", "tp"), P("ctx", "tp"), P("ctx", "tp"),
        P(), P(), P(), P(None, "tp"), P("tp", None), P("tp", None),
    )
    out_specs = P(("ctx", "tp"), None)
    return jax.shard_map(
        per_device, mesh=mesh, in_specs=in_specs, out_specs=out_specs, check_vma=False
    )
```

```python
import functools
import math

import jax
import jax.numpy as jnp
from jax import lax
from jax.experimental import pallas as pl
from jax.experimental.pallas import tpu as pltpu
from jax.sharding import PartitionSpec as P

HD = 128
TILE = 1024
neg_large = -1e30
eps_norm = 1e-06


def interval(table, first, rows):
    clips = table.shape[0] // 2

    def clip_of(pos):
        number = jnp.int32(0)
        for clip in range(clips - 1):
            number = number + (pos >= table[clip]).astype(jnp.int32)
        return number

    def start_of(number):
        return jnp.where(number == 0, 0, table[jnp.maximum(number - 1, 0)])

    low, high = clip_of(first), clip_of(first + rows - 1)
    end = jnp.where(table[clips + high] == 0, table[high], first + rows)
    whole_end = jnp.where(table[clips + low] == 0, table[low], first + 1)
    return start_of(low), end, start_of(high), whole_end


def attend_kernel(table, q_ref, k_ref, v_ref, out_ref, acc, peak, edges):
    step = pl.program_id(0)
    rows = q_ref.shape[0]
    clips = table.shape[0] // 2
    first = lax.axis_index("ctx") * rows
    some_low, some_high, whole_low, whole_high = interval(table, first, rows)
    tile = some_low // TILE + step
    factor = math.log2(math.e) / math.sqrt(HD)
    heads = q_ref.shape[1] // HD

    @pl.when(step == 0)
    def _():
        acc[...] = jnp.zeros_like(acc)
        peak[...] = jnp.full_like(peak, neg_large)
        pos = first + lax.broadcasted_iota(jnp.int32, (rows, HD), 0)
        start = jnp.zeros_like(pos)
        end = jnp.where(table[clips] == 0, table[0], pos + 1)
        for clip in range(1, clips):
            later = pos >= table[clip - 1]
            start = jnp.where(later, table[clip - 1], start)
            end = jnp.where(
                later, jnp.where(table[clips + clip] == 0, table[clip], pos + 1), end
            )
        edges[0] = start
        edges[1] = end

    def one_tile(masked):
        if masked:
            pos = tile * TILE + lax.broadcasted_iota(jnp.int32, (rows, TILE), 1)
            allowed = (pos >= edges[0][:, :1]) & (pos < edges[1][:, :1])
        ones = jnp.ones((TILE, HD), jnp.bfloat16)
        for head in range(heads):
            cols = slice(head * HD, (head + 1) * HD)
            scores = lax.dot_general(
                q_ref[:, cols], k_ref[:, cols], (((1,), (1,)), ((), ())),
                preferred_element_type=jnp.float32,
            )
            if masked:
                scores = jnp.where(allowed, scores, neg_large)
            old = peak[head]
            new = jnp.maximum(old, jnp.max(scores, axis=1, keepdims=True))
            weights = jnp.exp2((scores - new[:, :1]) * factor)
            if masked:
                weights = jnp.where(allowed, weights, 0.0)
            shrink = jnp.exp2((old - new) * factor)
            values = jnp.concatenate([v_ref[:, cols], ones], axis=1)
            added = jnp.dot(
                weights.astype(jnp.bfloat16), values, preferred_element_type=jnp.float32
            )
            acc[head] = acc[head] * jnp.concatenate([shrink, shrink], axis=1) + added
            peak[head] = new

    active = tile * TILE < some_high
    whole = (tile * TILE >= whole_low) & ((tile + 1) * TILE <= whole_high)

    @pl.when(active & whole)
    def _():
        one_tile(False)

    @pl.when(active & jnp.logical_not(whole))
    def _():
        one_tile(True)

    @pl.when(step == pl.num_programs(0) - 1)
    def _():
        for head in range(heads):
            out_ref[:, head * HD:(head + 1) * HD] = (
                acc[head][:, :HD] / acc[head][:, HD:]
            ).astype(out_ref.dtype)


def attention(queries, keys, values, table):
    rows, width = queries.shape
    tiles = keys.shape[0] // TILE

    def kv_map(step, table):
        low, high, _, _ = interval(table, lax.axis_index("ctx") * rows, rows)
        return (jnp.minimum(low // TILE + step, (high - 1) // TILE), 0)

    def fixed(step, table):
        return (0, 0)

    return pl.pallas_call(
        attend_kernel,
        out_shape=jax.ShapeDtypeStruct((rows, width), jnp.bfloat16),
        grid_spec=pltpu.PrefetchScalarGridSpec(
            num_scalar_prefetch=1,
            grid=(tiles,),
            in_specs=[
                pl.BlockSpec((rows, width), fixed),
                pl.BlockSpec((TILE, width), kv_map),
                pl.BlockSpec((TILE, width), kv_map),
            ],
            out_specs=pl.BlockSpec((rows, width), fixed),
            scratch_shapes=[
                pltpu.VMEM((width // HD, rows, 2 * HD), jnp.float32),
                pltpu.VMEM((width // HD, rows, HD), jnp.float32),
                pltpu.VMEM((2, rows, HD), jnp.int32),
            ],
        ),
        compiler_params=pltpu.CompilerParams(vmem_limit_bytes=60 << 20),
        cost_estimate=pl.CostEstimate(
            flops=8 * rows * keys.shape[0] * width,
            bytes_accessed=4 * keys.shape[0] * width,
            transcendentals=rows * keys.shape[0] * width // HD,
        ),
        name="attend",
    )(table, queries, keys, values)


def remote(src, dst, send_sem, recv_sem, where):
    return pltpu.make_async_remote_copy(
        src_ref=src, dst_ref=dst, send_sem=send_sem, recv_sem=recv_sem,
        device_id=where, device_id_type=pl.DeviceIdType.MESH,
    )


def greet(places):
    barrier = pltpu.get_barrier_semaphore()
    for place in places:
        pl.semaphore_signal(
            barrier, inc=1, device_id=place, device_id_type=pl.DeviceIdType.MESH
        )
    pl.semaphore_wait(barrier, len(places))


Y, Z, CORES = 4, 4, 2
X, HI = 4, 2
COPIES = 2 * (Z - 1) + 6 * Z + 2 * Y * Z + 12


LN_ROWS = 32


def gather_kernel(
    ends_ref, modulation, tokens, keys, values, w_in_hbm, w_out_hbm,
    whole, key_all, value_all, part,
    w_in, w_out, modulated, hidden, halfway, stage, send, recv, local,
):
    rows = keys.shape[0]
    me = lax.axis_index("ctx")
    y, z, core = me // (Z * CORES), me // CORES % Z, me % CORES
    pair = (key_all, value_all)
    own = (keys, values)

    def index(dy, dz, flip=False):
        other = 1 - core if flip else core
        return ((y + dy + Y) % Y * Z + (z + dz + Z) % Z) * CORES + other

    def slot(which, dy, dz, flip=False):
        start = pl.multiple_of(index(dy, dz, flip) * rows, rows)
        return pair[which].at[pl.ds(start, rows)]

    def at(dy, dz, flip=False):
        return {"ctx": index(dy, dz, flip)}

    apart = (0, 1 - 2 * (z % 2), 2 - 4 * (z // 2), 3 - 2 * z)

    lead = lax.axis_index("tp")
    x, hi = lead // HI, lead % HI
    half, wide = tokens.shape[0] // 2, tokens.shape[1]

    def column(dx, flip=False):
        return (x + dx + X) % X * HI + (1 - hi if flip else hi)

    def strip(dx, flip=False, part=None):
        cols = pl.ds(pl.multiple_of(column(dx, flip) * wide, wide), wide)
        if part is None:
            return whole.at[:, cols]
        return whole.at[pl.ds(part * half, half), cols]

    right, left = {"tp": column(1)}, {"tp": column(-1)}
    depth = hi * Z + z

    def along(steps):
        place = (depth + steps + Z * HI) % (Z * HI)
        return {"ctx": (y * Z + place % Z) * CORES + core, "tp": x * HI + place // Z}

    up, down = along(2), along(-2)
    greet(
        [at(0, apart[r]) for r in range(1, Z)]
        + [at(1, 0), at(-1, 0), at(0, 0, True), right, left, up, down]
    )

    def origin(steps, part):
        lead_there = along(steps)["tp"]
        cols = pl.ds(pl.multiple_of(lead_there * wide, wide), wide)
        return whole.at[pl.ds(part * half, half), cols]
    started = []
    made = [0]

    def pass_on(src, dst, where):
        number = made[0]
        made[0] += 1
        copy = remote(src, dst, send.at[number], recv.at[number], where)
        copy.start()
        started.append(copy)
        return copy

    def swap(r):
        return [
            pass_on(own[w], slot(w, 0, 0), at(0, apart[r])) for w in (0, 1)
        ]

    to_z = [None, swap(1), None, None]
    sides = [pass_on(tokens, strip(0), right), pass_on(tokens, strip(0), left)]

    def make(src, which, owner, target):
        return pass_on(src, slot(which, *owner), at(*target))

    enter = [pltpu.make_async_copy(own[w], stage.at[w], local.at[w]) for w in (0, 1)]
    leave = [
        pltpu.make_async_copy(stage.at[w], slot(w, 0, 0), local.at[5 + w]) for w in (0, 1)
    ]
    stay = [pltpu.make_async_copy(tokens, strip(0), local.at[2])]
    weights = [
        pltpu.make_async_copy(w_in_hbm, w_in, local.at[3]),
        pltpu.make_async_copy(w_out_hbm, w_out, local.at[4]),
    ]
    stay += weights
    for copy in enter + stay:
        copy.start()
    near = [[None] * 4 for _ in range(Z)]
    far = [[None] * 2 for _ in range(Z)]
    to_core = []

    def spread(r):
        dz = apart[r]
        for w in (0, 1):
            src = own[w] if r == 0 else slot(w, 0, dz)
            near[r][w] = make(src, w, (0, dz), (1, 0))
            near[r][2 + w] = make(src, w, (0, dz), (-1, 0))
            to_core.append(make(src, w, (0, dz), (0, 0, True)))

    def relay(r):
        dz = apart[r]
        near[r][0].wait_recv()
        far[r][0] = make(slot(0, -1, dz), 0, (-1, dz), (1, 0))
        near[r][3].wait_recv()
        far[r][1] = make(slot(1, 1, dz), 1, (1, dz), (-1, 0))
        near[r][1].wait_recv()
        near[r][2].wait_recv()
        for w in (0, 1):
            for dy in (-1, 1):
                to_core.append(make(slot(w, dy, dz), w, (dy, dz), (0, 0, True)))

    def finish(r):
        for w in (0, 1):
            far[r][w].wait_recv()
            to_core.append(make(slot(w, 2, apart[r]), w, (2, apart[r]), (0, 0, True)))

    def arrived(copies):
        for copy in copies:
            copy.wait_recv()

    spread(0)

    def tokens_far(copies, flip):
        arrived(copies)
        return [
            pass_on(strip(-1, flip, 0), strip(-1, flip, 0), right),
            pass_on(strip(1, flip, 1), strip(1, flip, 1), left),
        ]

    def normalize(first, last):
        @pl.loop(first // LN_ROWS, last // LN_ROWS)
        def _(block):
            start = pl.multiple_of(block * LN_ROWS, LN_ROWS)
            values = whole[pl.ds(start, LN_ROWS), :].astype(jnp.float32)
            centred = values - jnp.mean(values, axis=1, keepdims=True)
            variance = jnp.mean(centred * centred, axis=1, keepdims=True)
            normed = centred * lax.rsqrt(variance + eps_norm)
            pos = me * rows + start + lax.broadcasted_iota(jnp.int32, (LN_ROWS, 1), 0)
            shift = jnp.broadcast_to(modulation[0, 0:1, :], normed.shape)
            scale = jnp.broadcast_to(modulation[1, 0:1, :], normed.shape)
            for clip in range(1, modulation.shape[1]):
                later = pos >= ends_ref[clip - 1]
                shift = jnp.where(later, modulation[0, clip:clip + 1, :], shift)
                scale = jnp.where(later, modulation[1, clip:clip + 1, :], scale)
            modulated[pl.ds(start, LN_ROWS), :] = (normed * (1.0 + scale) + shift).astype(
                modulated.dtype
            )

    def project(source, weight, target, width, finish_tile):
        @pl.loop(0, weight.shape[1] // width)
        def _(block):
            cols = pl.ds(pl.multiple_of(block * width, width), width)
            target[:, cols] = finish_tile(
                jnp.dot(source[...], weight[:, cols], preferred_element_type=jnp.float32)
            ).astype(target.dtype)

    arrived(to_z[1])
    to_z[2] = swap(2)
    spread(1)
    over = [
        pass_on(tokens.at[pl.ds(0, half)], halfway.at[0], up),
        pass_on(tokens.at[pl.ds(half, half)], halfway.at[1], down),
    ]
    for copy in enter:
        copy.wait()
    for copy in leave:
        copy.start()
    ends = tokens_far(sides, False)
    relay(0)
    arrived(over)
    over = [
        pass_on(halfway.at[0], origin(-2, 0), up),
        pass_on(halfway.at[1], origin(2, 1), down),
    ]
    arrived(to_z[2])
    to_z[3] = swap(3)
    spread(2)
    relay(1)
    finish(0)
    arrived(over)
    sides = [pass_on(strip(0, True), strip(0, True), to) for to in (right, left)]
    arrived(to_z[3])
    spread(3)
    ends += tokens_far(sides, True)
    relay(2)
    finish(1)
    arrived(ends)
    for copy in stay:
        copy.wait()
    normalize(0, rows)
    relay(3)
    finish(2)
    project(
        modulated, w_in, hidden, 256, functools.partial(jax.nn.gelu, approximate=True)
    )
    finish(3)
    project(hidden, w_out, part, 512, lambda tile: tile)
    for copy in leave:
        copy.wait()
    for copy in to_core:
        copy.wait_recv()
    for copy in started:
        copy.wait_send()


def gather_rows(clip_end, modulation, tokens, keys, values, w_in, w_out, devices, leads):
    rows, width = keys.shape
    hbm = pl.BlockSpec(memory_space=pl.ANY)
    vmem = pl.BlockSpec(memory_space=pltpu.VMEM)
    gathered = jax.ShapeDtypeStruct((rows * devices, width), keys.dtype)
    return pl.pallas_call(
        gather_kernel,
        out_shape=(
            jax.ShapeDtypeStruct((rows, tokens.shape[1] * leads), tokens.dtype),
            gathered,
            gathered,
            jax.ShapeDtypeStruct((rows, w_out.shape[1]), jnp.float32),
        ),
        in_specs=[pl.BlockSpec(memory_space=pltpu.SMEM), vmem, hbm, hbm, hbm, hbm, hbm],
        out_specs=(vmem, hbm, hbm, vmem),
        scratch_shapes=[
            pltpu.VMEM(w_in.shape, w_in.dtype),
            pltpu.VMEM(w_out.shape, w_out.dtype),
            pltpu.VMEM((rows, w_in.shape[0]), jnp.bfloat16),
            pltpu.VMEM((rows, w_in.shape[1]), jnp.bfloat16),
            pltpu.VMEM((2, rows // 2, tokens.shape[1]), tokens.dtype),
            pltpu.VMEM((2,) + keys.shape, keys.dtype),
            pltpu.SemaphoreType.DMA((COPIES,)),
            pltpu.SemaphoreType.DMA((COPIES,)),
            pltpu.SemaphoreType.DMA((7,)),
        ],
        compiler_params=pltpu.CompilerParams(
            collective_id=0, has_side_effects=True, vmem_limit_bytes=60 << 20
        ),
        name="gather_all",
    )(clip_end, modulation, tokens, keys, values, w_in, w_out)


CHUNKS = 4


def reduce_kernel(
    ends_ref, modulation, whole, part,
    out, held, relayed, outgoing, incoming, sums, residual, send, recv, local,
):
    rows = part.shape[0] // (X * HI)
    wide = part.shape[1] // CHUNKS
    me = lax.axis_index("tp")
    x, hi = me // HI, me % HI
    right = {"tp": (x + 1) % X * HI + hi}
    left = {"tp": (x + X - 1) % X * HI + hi}
    across = {"tp": x * HI + 1 - hi}
    greet([left, right, across])
    mine = pl.ds(pl.multiple_of(me * rows, rows), rows)
    fetch = pltpu.make_async_copy(whole.at[mine], residual, local)
    fetch.start()

    def piece(dx, first, count, chunk):
        start = pl.multiple_of(((x + dx) % X * HI + first) * rows, rows)
        return part.at[pl.ds(start, count * rows), pl.ds(chunk * wide, wide)]

    def cols(chunk):
        return slice(chunk * wide, (chunk + 1) * wide)

    def copy(src, dst, chunk, kind, where):
        made = remote(src, dst, send.at[chunk, kind], recv.at[chunk, kind], where)
        made.start()
        return made

    copies = [[None] * 7 for _ in range(CHUNKS)]

    def begin(c):
        mine = copies[c]
        mine[2] = copy(piece(2, 0, 1, c), relayed.at[0, c], c, 2, right)
        mine[3] = copy(piece(2, 1, 1, c), relayed.at[1, c], c, 3, left)
        mine[0] = copy(piece(1, 0, 2, c), held.at[0, c], c, 0, right)
        mine[1] = copy(piece(3, 0, 2, c), held.at[1, c], c, 1, left)

    def forward(c):
        mine = copies[c]
        mine[2].wait_recv()
        mine[4] = copy(relayed.at[0, c], held.at[2, c, pl.ds(0, rows)], c, 4, right)
        mine[3].wait_recv()
        mine[5] = copy(relayed.at[1, c], held.at[2, c, pl.ds(rows, rows)], c, 5, left)

    def total(c, half):
        start = pl.multiple_of(half * rows, rows)
        own = pl.multiple_of((x * HI + half) * rows, rows)
        result = part[pl.ds(own, rows), cols(c)].astype(jnp.float32)
        for source in range(3):
            result += held[source, c, pl.ds(start, rows)].astype(jnp.float32)
        return result

    def combine(c):
        mine = copies[c]
        for kind in (0, 1, 4, 5):
            mine[kind].wait_recv()
        outgoing[c] = total(c, 1 - hi).astype(jnp.bfloat16)
        sums[c] = total(c, hi)
        mine[6] = copy(outgoing.at[c], incoming.at[c], c, 6, across)

    for c in range(CHUNKS):
        begin(c)
    for c in range(CHUNKS):
        forward(c)
        if c > 0:
            combine(c - 1)
    combine(CHUNKS - 1)
    fetch.wait()
    first = (lax.axis_index("ctx") * X * HI + me) * rows
    pos = first + lax.broadcasted_iota(jnp.int32, (rows, 1), 0)
    for c in range(CHUNKS):
        copies[c][6].wait_recv()
        branch = sums[c] + incoming[c].astype(jnp.float32)
        gate = jnp.broadcast_to(modulation[2, 0:1, cols(c)], branch.shape)
        for clip in range(1, modulation.shape[1]):
            later = pos >= ends_ref[clip - 1]
            gate = jnp.where(later, modulation[2, clip:clip + 1, cols(c)], gate)
        out[:, cols(c)] = residual[:, cols(c)].astype(jnp.float32) + gate * branch
    for mine in copies:
        for made in mine:
            made.wait_send()


def reduce_rows(clip_end, modulation, whole, part):
    rows, width = part.shape[0] // (X * HI), part.shape[1]
    wide = width // CHUNKS
    vmem = pl.BlockSpec(memory_space=pltpu.VMEM)
    return pl.pallas_call(
        reduce_kernel,
        out_shape=jax.ShapeDtypeStruct((rows, width), jnp.float32),
        in_specs=[
            pl.BlockSpec(memory_space=pltpu.SMEM), vmem, pl.BlockSpec(memory_space=pl.ANY), vmem
        ],
        out_specs=vmem,
        scratch_shapes=[
            pltpu.VMEM((3, CHUNKS, HI * rows, wide), jnp.bfloat16),
            pltpu.VMEM((2, CHUNKS, rows, wide), jnp.bfloat16),
            pltpu.VMEM((CHUNKS, rows, wide), jnp.bfloat16),
            pltpu.VMEM((CHUNKS, rows, wide), jnp.bfloat16),
            pltpu.VMEM((CHUNKS, rows, wide), jnp.float32),
            pltpu.VMEM((rows, width), jnp.bfloat16),
            pltpu.SemaphoreType.DMA((CHUNKS, 7)),
            pltpu.SemaphoreType.DMA((CHUNKS, 7)),
            pltpu.SemaphoreType.DMA,
        ],
        compiler_params=pltpu.CompilerParams(
            collective_id=1, has_side_effects=True, vmem_limit_bytes=24 << 20
        ),
        cost_estimate=pl.CostEstimate(flops=0, bytes_accessed=100_000_000, transcendentals=0),
        name="reduce_branch",
    )(clip_end, modulation, whole, part)


def per_device(
    tokens, queries, key_rows, value_rows, clip_ids, causal, modulation, w_mlp, w_attn_out, w_mlp_out
):
    local_rows = queries.shape[0]
    tp_size = lax.axis_size("tp")
    clips = causal.shape[0]
    numbers = jnp.arange(clips, dtype=jnp.int32)
    clip_end = jnp.sum((clip_ids[None, :] <= numbers[:, None]).astype(jnp.int32), axis=1)
    whole_rows, key_all, value_all, mlp_part = gather_rows(
        clip_end, modulation, tokens, key_rows, value_rows, w_mlp, w_mlp_out,
        lax.axis_size("ctx"), tp_size,
    )
    attended = attention(queries, key_all, value_all, jnp.concatenate([clip_end, causal]))
    part = jnp.dot(attended, w_attn_out, preferred_element_type=jnp.float32) + mlp_part
    return reduce_rows(clip_end, modulation, whole_rows, part.astype(jnp.bfloat16))


def solution(mesh):
    in_specs = (
        P("ctx", "tp"), P("ctx", "tp"), P("ctx", "tp"), P("ctx", "tp"),
        P(), P(), P(), P(None, "tp"), P("tp", None), P("tp", None),
    )
    out_specs = P(("ctx", "tp"), None)
    return jax.shard_map(
        per_device, mesh=mesh, in_specs=in_specs, out_specs=out_specs, check_vma=False
    )
```

```python
import functools
import math

import jax
import jax.numpy as jnp
from jax import lax
from jax.experimental import pallas as pl
from jax.experimental.pallas import tpu as pltpu
from jax.sharding import PartitionSpec as P

HD = 128
TILE = 1024
neg_large = -1e30
eps_norm = 1e-06


def interval(table, first, rows):
    clips = table.shape[0] // 2

    def clip_of(pos):
        number = jnp.int32(0)
        for clip in range(clips - 1):
            number = number + (pos >= table[clip]).astype(jnp.int32)
        return number

    def start_of(number):
        return jnp.where(number == 0, 0, table[jnp.maximum(number - 1, 0)])

    low, high = clip_of(first), clip_of(first + rows - 1)
    end = jnp.where(table[clips + high] == 0, table[high], first + rows)
    whole_end = jnp.where(table[clips + low] == 0, table[low], first + 1)
    return start_of(low), end, start_of(high), whole_end


def attend_kernel(table, q_ref, k_ref, v_ref, out_ref, acc, peak, edges):
    step = pl.program_id(0)
    rows = q_ref.shape[0]
    clips = table.shape[0] // 2
    first = lax.axis_index("ctx") * rows
    some_low, some_high, whole_low, whole_high = interval(table, first, rows)
    tile = some_low // TILE + step
    factor = math.log2(math.e) / math.sqrt(HD)
    heads = q_ref.shape[1] // HD

    @pl.when(step == 0)
    def _():
        acc[...] = jnp.zeros_like(acc)
        peak[...] = jnp.full_like(peak, neg_large)
        pos = first + lax.broadcasted_iota(jnp.int32, (rows, HD), 0)
        start = jnp.zeros_like(pos)
        end = jnp.where(table[clips] == 0, table[0], pos + 1)
        for clip in range(1, clips):
            later = pos >= table[clip - 1]
            start = jnp.where(later, table[clip - 1], start)
            end = jnp.where(
                later, jnp.where(table[clips + clip] == 0, table[clip], pos + 1), end
            )
        edges[0] = start
        edges[1] = end

    def one_tile(masked):
        if masked:
            pos = tile * TILE + lax.broadcasted_iota(jnp.int32, (rows, TILE), 1)
            allowed = (pos >= edges[0][:, :1]) & (pos < edges[1][:, :1])
        ones = jnp.ones((TILE, HD), jnp.bfloat16)
        for head in range(heads):
            cols = slice(head * HD, (head + 1) * HD)
            scores = lax.dot_general(
                q_ref[:, cols], k_ref[:, cols], (((1,), (1,)), ((), ())),
                preferred_element_type=jnp.float32,
            )
            if masked:
                scores = jnp.where(allowed, scores, neg_large)
            old = peak[head]
            new = jnp.maximum(old, jnp.max(scores, axis=1, keepdims=True))
            weights = jnp.exp2((scores - new[:, :1]) * factor)
            if masked:
                weights = jnp.where(allowed, weights, 0.0)
            shrink = jnp.exp2((old - new) * factor)
            values = jnp.concatenate([v_ref[:, cols], ones], axis=1)
            added = jnp.dot(
                weights.astype(jnp.bfloat16), values, preferred_element_type=jnp.float32
            )
            acc[head] = acc[head] * jnp.concatenate([shrink, shrink], axis=1) + added
            peak[head] = new

    active = tile * TILE < some_high
    whole = (tile * TILE >= whole_low) & ((tile + 1) * TILE <= whole_high)

    @pl.when(active & whole)
    def _():
        one_tile(False)

    @pl.when(active & jnp.logical_not(whole))
    def _():
        one_tile(True)

    @pl.when(step == pl.num_programs(0) - 1)
    def _():
        for head in range(heads):
            out_ref[:, head * HD:(head + 1) * HD] = (
                acc[head][:, :HD] / acc[head][:, HD:]
            ).astype(out_ref.dtype)


def attention(queries, keys, values, table):
    rows, width = queries.shape
    tiles = keys.shape[0] // TILE

    def kv_map(step, table):
        low, high, _, _ = interval(table, lax.axis_index("ctx") * rows, rows)
        return (jnp.minimum(low // TILE + step, (high - 1) // TILE), 0)

    def fixed(step, table):
        return (0, 0)

    return pl.pallas_call(
        attend_kernel,
        out_shape=jax.ShapeDtypeStruct((rows, width), jnp.bfloat16),
        grid_spec=pltpu.PrefetchScalarGridSpec(
            num_scalar_prefetch=1,
            grid=(tiles,),
            in_specs=[
                pl.BlockSpec((rows, width), fixed),
                pl.BlockSpec((TILE, width), kv_map),
                pl.BlockSpec((TILE, width), kv_map),
            ],
            out_specs=pl.BlockSpec((rows, width), fixed),
            scratch_shapes=[
                pltpu.VMEM((width // HD, rows, 2 * HD), jnp.float32),
                pltpu.VMEM((width // HD, rows, HD), jnp.float32),
                pltpu.VMEM((2, rows, HD), jnp.int32),
            ],
        ),
        compiler_params=pltpu.CompilerParams(vmem_limit_bytes=60 << 20),
        cost_estimate=pl.CostEstimate(
            flops=8 * rows * keys.shape[0] * width,
            bytes_accessed=4 * keys.shape[0] * width,
            transcendentals=rows * keys.shape[0] * width // HD,
        ),
        name="attend",
    )(table, queries, keys, values)


def remote(src, dst, send_sem, recv_sem, where):
    return pltpu.make_async_remote_copy(
        src_ref=src, dst_ref=dst, send_sem=send_sem, recv_sem=recv_sem,
        device_id=where, device_id_type=pl.DeviceIdType.MESH,
    )


def greet(places):
    barrier = pltpu.get_barrier_semaphore()
    for place in places:
        pl.semaphore_signal(
            barrier, inc=1, device_id=place, device_id_type=pl.DeviceIdType.MESH
        )
    pl.semaphore_wait(barrier, len(places))


Y, Z, CORES = 4, 4, 2
X, HI = 4, 2
COPIES = 2 * (Z - 1) + 6 * Z + 2 * Y * Z + 12


LN_ROWS = 32


def gather_kernel(
    ends_ref, modulation, tokens, keys, values, w_in_hbm, w_out_hbm,
    whole, key_all, value_all, part,
    w_in, w_out, modulated, hidden, halfway, stage, send, recv, local,
):
    rows = keys.shape[0]
    me = lax.axis_index("ctx")
    y, z, core = me // (Z * CORES), me // CORES % Z, me % CORES
    pair = (key_all, value_all)
    own = (keys, values)

    def index(dy, dz, flip=False):
        other = 1 - core if flip else core
        return ((y + dy + Y) % Y * Z + (z + dz + Z) % Z) * CORES + other

    def slot(which, dy, dz, flip=False):
        start = pl.multiple_of(index(dy, dz, flip) * rows, rows)
        return pair[which].at[pl.ds(start, rows)]

    def at(dy, dz, flip=False):
        return {"ctx": index(dy, dz, flip)}

    apart = (0, 1 - 2 * (z % 2), 2 - 4 * (z // 2), 3 - 2 * z)

    lead = lax.axis_index("tp")
    x, hi = lead // HI, lead % HI
    half, wide = tokens.shape[0] // 2, tokens.shape[1]

    def column(dx, flip=False):
        return (x + dx + X) % X * HI + (1 - hi if flip else hi)

    def strip(dx, flip=False, part=None):
        cols = pl.ds(pl.multiple_of(column(dx, flip) * wide, wide), wide)
        if part is None:
            return whole.at[:, cols]
        return whole.at[pl.ds(part * half, half), cols]

    right, left = {"tp": column(1)}, {"tp": column(-1)}
    depth = hi * Z + z

    def along(steps):
        place = (depth + steps + Z * HI) % (Z * HI)
        return {"ctx": (y * Z + place % Z) * CORES + core, "tp": x * HI + place // Z}

    up, down = along(2), along(-2)
    greet(
        [at(0, apart[r]) for r in range(1, Z)]
        + [at(1, 0), at(-1, 0), at(0, 0, True), right, left, up, down]
    )

    def origin(steps, part):
        lead_there = along(steps)["tp"]
        cols = pl.ds(pl.multiple_of(lead_there * wide, wide), wide)
        return whole.at[pl.ds(part * half, half), cols]
    started = []
    made = [0]

    def pass_on(src, dst, where):
        number = made[0]
        made[0] += 1
        copy = remote(src, dst, send.at[number], recv.at[number], where)
        copy.start()
        started.append(copy)
        return copy

    def swap(r):
        return [
            pass_on(own[w], slot(w, 0, 0), at(0, apart[r])) for w in (0, 1)
        ]

    to_z = [None, swap(1), None, None]
    over = [
        pass_on(tokens.at[pl.ds(0, half)], halfway.at[0], up),
        pass_on(tokens.at[pl.ds(half, half)], halfway.at[1], down),
    ]
    sides = [pass_on(tokens, strip(0), right), pass_on(tokens, strip(0), left)]

    def make(src, which, owner, target):
        return pass_on(src, slot(which, *owner), at(*target))

    enter = [pltpu.make_async_copy(own[w], stage.at[w], local.at[w]) for w in (0, 1)]
    leave = [
        pltpu.make_async_copy(stage.at[w], slot(w, 0, 0), local.at[5 + w]) for w in (0, 1)
    ]
    stay = [pltpu.make_async_copy(tokens, strip(0), local.at[2])]
    weights = [
        pltpu.make_async_copy(w_in_hbm, w_in, local.at[3]),
        pltpu.make_async_copy(w_out_hbm, w_out, local.at[4]),
    ]
    stay += weights
    for copy in enter + stay:
        copy.start()
    near = [[None] * 4 for _ in range(Z)]
    far = [[None] * 2 for _ in range(Z)]
    to_core = []

    def spread(r):
        dz = apart[r]
        for w in (0, 1):
            src = own[w] if r == 0 else slot(w, 0, dz)
            near[r][w] = make(src, w, (0, dz), (1, 0))
            near[r][2 + w] = make(src, w, (0, dz), (-1, 0))
            to_core.append(make(src, w, (0, dz), (0, 0, True)))

    def relay(r):
        dz = apart[r]
        near[r][0].wait_recv()
        far[r][0] = make(slot(0, -1, dz), 0, (-1, dz), (1, 0))
        near[r][3].wait_recv()
        far[r][1] = make(slot(1, 1, dz), 1, (1, dz), (-1, 0))
        near[r][1].wait_recv()
        near[r][2].wait_recv()
        for w in (0, 1):
            for dy in (-1, 1):
                to_core.append(make(slot(w, dy, dz), w, (dy, dz), (0, 0, True)))

    def finish(r):
        for w in (0, 1):
            far[r][w].wait_recv()
            to_core.append(make(slot(w, 2, apart[r]), w, (2, apart[r]), (0, 0, True)))

    def arrived(copies):
        for copy in copies:
            copy.wait_recv()

    spread(0)

    def tokens_far(copies, flip):
        arrived(copies)
        return [
            pass_on(strip(-1, flip, 0), strip(-1, flip, 0), right),
            pass_on(strip(1, flip, 1), strip(1, flip, 1), left),
        ]

    def normalize(first, last):
        @pl.loop(first // LN_ROWS, last // LN_ROWS)
        def _(block):
            start = pl.multiple_of(block * LN_ROWS, LN_ROWS)
            values = whole[pl.ds(start, LN_ROWS), :].astype(jnp.float32)
            centred = values - jnp.mean(values, axis=1, keepdims=True)
            variance = jnp.mean(centred * centred, axis=1, keepdims=True)
            normed = centred * lax.rsqrt(variance + eps_norm)
            pos = me * rows + start + lax.broadcasted_iota(jnp.int32, (LN_ROWS, 1), 0)
            shift = jnp.broadcast_to(modulation[0, 0:1, :], normed.shape)
            scale = jnp.broadcast_to(modulation[1, 0:1, :], normed.shape)
            for clip in range(1, modulation.shape[1]):
                later = pos >= ends_ref[clip - 1]
                shift = jnp.where(later, modulation[0, clip:clip + 1, :], shift)
                scale = jnp.where(later, modulation[1, clip:clip + 1, :], scale)
            modulated[pl.ds(start, LN_ROWS), :] = (normed * (1.0 + scale) + shift).astype(
                modulated.dtype
            )

    def project(source, weight, target, width, finish_tile):
        @pl.loop(0, weight.shape[1] // width)
        def _(block):
            cols = pl.ds(pl.multiple_of(block * width, width), width)
            target[:, cols] = finish_tile(
                jnp.dot(source[...], weight[:, cols], preferred_element_type=jnp.float32)
            ).astype(target.dtype)

    arrived(to_z[1])
    to_z[2] = swap(2)
    spread(1)
    for copy in enter:
        copy.wait()
    for copy in leave:
        copy.start()
    ends = tokens_far(sides, False)
    arrived(over)
    over = [
        pass_on(halfway.at[0], origin(-2, 0), up),
        pass_on(halfway.at[1], origin(2, 1), down),
    ]
    relay(0)
    arrived(over)
    sides = [pass_on(strip(0, True), strip(0, True), to) for to in (right, left)]
    arrived(to_z[2])
    to_z[3] = swap(3)
    spread(2)
    relay(1)
    ends += tokens_far(sides, True)
    finish(0)
    arrived(ends)
    for copy in stay:
        copy.wait()
    normalize(0, rows // 2)
    arrived(to_z[3])
    spread(3)
    relay(2)
    normalize(rows // 2, rows)
    finish(1)
    project(
        modulated, w_in, hidden, 256, functools.partial(jax.nn.gelu, approximate=True)
    )
    relay(3)
    finish(2)
    project(hidden, w_out, part, 512, lambda tile: tile)
    finish(3)
    for copy in leave:
        copy.wait()
    for copy in to_core:
        copy.wait_recv()
    for copy in started:
        copy.wait_send()


def gather_rows(clip_end, modulation, tokens, keys, values, w_in, w_out, devices, leads):
    rows, width = keys.shape
    hbm = pl.BlockSpec(memory_space=pl.ANY)
    vmem = pl.BlockSpec(memory_space=pltpu.VMEM)
    gathered = jax.ShapeDtypeStruct((rows * devices, width), keys.dtype)
    return pl.pallas_call(
        gather_kernel,
        out_shape=(
            jax.ShapeDtypeStruct((rows, tokens.shape[1] * leads), tokens.dtype),
            gathered,
            gathered,
            jax.ShapeDtypeStruct((rows, w_out.shape[1]), jnp.float32),
        ),
        in_specs=[pl.BlockSpec(memory_space=pltpu.SMEM), vmem, hbm, hbm, hbm, hbm, hbm],
        out_specs=(vmem, hbm, hbm, vmem),
        scratch_shapes=[
            pltpu.VMEM(w_in.shape, w_in.dtype),
            pltpu.VMEM(w_out.shape, w_out.dtype),
            pltpu.VMEM((rows, w_in.shape[0]), jnp.bfloat16),
            pltpu.VMEM((rows, w_in.shape[1]), jnp.bfloat16),
            pltpu.VMEM((2, rows // 2, tokens.shape[1]), tokens.dtype),
            pltpu.VMEM((2,) + keys.shape, keys.dtype),
            pltpu.SemaphoreType.DMA((COPIES,)),
            pltpu.SemaphoreType.DMA((COPIES,)),
            pltpu.SemaphoreType.DMA((7,)),
        ],
        compiler_params=pltpu.CompilerParams(
            collective_id=0, has_side_effects=True, vmem_limit_bytes=60 << 20
        ),
        name="gather_all",
    )(clip_end, modulation, tokens, keys, values, w_in, w_out)


CHUNKS = 4


def reduce_kernel(
    ends_ref, modulation, whole, part,
    out, held, relayed, outgoing, incoming, sums, residual, send, recv, local,
):
    rows = part.shape[0] // (X * HI)
    wide = part.shape[1] // CHUNKS
    me = lax.axis_index("tp")
    x, hi = me // HI, me % HI
    right = {"tp": (x + 1) % X * HI + hi}
    left = {"tp": (x + X - 1) % X * HI + hi}
    across = {"tp": x * HI + 1 - hi}
    greet([left, right, across])
    mine = pl.ds(pl.multiple_of(me * rows, rows), rows)
    fetch = pltpu.make_async_copy(whole.at[mine], residual, local)
    fetch.start()

    def piece(dx, first, count, chunk):
        start = pl.multiple_of(((x + dx) % X * HI + first) * rows, rows)
        return part.at[pl.ds(start, count * rows), pl.ds(chunk * wide, wide)]

    def cols(chunk):
        return slice(chunk * wide, (chunk + 1) * wide)

    def copy(src, dst, chunk, kind, where):
        made = remote(src, dst, send.at[chunk, kind], recv.at[chunk, kind], where)
        made.start()
        return made

    copies = [[None] * 7 for _ in range(CHUNKS)]

    def begin(c):
        mine = copies[c]
        mine[2] = copy(piece(2, 0, 1, c), relayed.at[0, c], c, 2, right)
        mine[3] = copy(piece(2, 1, 1, c), relayed.at[1, c], c, 3, left)
        mine[0] = copy(piece(1, 0, 2, c), held.at[0, c], c, 0, right)
        mine[1] = copy(piece(3, 0, 2, c), held.at[1, c], c, 1, left)

    def forward(c):
        mine = copies[c]
        mine[2].wait_recv()
        mine[4] = copy(relayed.at[0, c], held.at[2, c, pl.ds(0, rows)], c, 4, right)
        mine[3].wait_recv()
        mine[5] = copy(relayed.at[1, c], held.at[2, c, pl.ds(rows, rows)], c, 5, left)

    def total(c, half):
        start = pl.multiple_of(half * rows, rows)
        own = pl.multiple_of((x * HI + half) * rows, rows)
        result = part[pl.ds(own, rows), cols(c)].astype(jnp.float32)
        for source in range(3):
            result += held[source, c, pl.ds(start, rows)].astype(jnp.float32)
        return result

    def combine(c):
        mine = copies[c]
        for kind in (0, 1, 4, 5):
            mine[kind].wait_recv()
        outgoing[c] = total(c, 1 - hi).astype(jnp.bfloat16)
        sums[c] = total(c, hi)
        mine[6] = copy(outgoing.at[c], incoming.at[c], c, 6, across)

    for c in range(CHUNKS):
        begin(c)
    for c in range(CHUNKS):
        forward(c)
        if c > 0:
            combine(c - 1)
    combine(CHUNKS - 1)
    fetch.wait()
    first = (lax.axis_index("ctx") * X * HI + me) * rows
    pos = first + lax.broadcasted_iota(jnp.int32, (rows, 1), 0)
    for c in range(CHUNKS):
        copies[c][6].wait_recv()
        branch = sums[c] + incoming[c].astype(jnp.float32)
        gate = jnp.broadcast_to(modulation[2, 0:1, cols(c)], branch.shape)
        for clip in range(1, modulation.shape[1]):
            later = pos >= ends_ref[clip - 1]
            gate = jnp.where(later, modulation[2, clip:clip + 1, cols(c)], gate)
        out[:, cols(c)] = residual[:, cols(c)].astype(jnp.float32) + gate * branch
    for mine in copies:
        for made in mine:
            made.wait_send()


def reduce_rows(clip_end, modulation, whole, part):
    rows, width = part.shape[0] // (X * HI), part.shape[1]
    wide = width // CHUNKS
    vmem = pl.BlockSpec(memory_space=pltpu.VMEM)
    return pl.pallas_call(
        reduce_kernel,
        out_shape=jax.ShapeDtypeStruct((rows, width), jnp.float32),
        in_specs=[
            pl.BlockSpec(memory_space=pltpu.SMEM), vmem, pl.BlockSpec(memory_space=pl.ANY), vmem
        ],
        out_specs=vmem,
        scratch_shapes=[
            pltpu.VMEM((3, CHUNKS, HI * rows, wide), jnp.bfloat16),
            pltpu.VMEM((2, CHUNKS, rows, wide), jnp.bfloat16),
            pltpu.VMEM((CHUNKS, rows, wide), jnp.bfloat16),
            pltpu.VMEM((CHUNKS, rows, wide), jnp.bfloat16),
            pltpu.VMEM((CHUNKS, rows, wide), jnp.float32),
            pltpu.VMEM((rows, width), jnp.bfloat16),
            pltpu.SemaphoreType.DMA((CHUNKS, 7)),
            pltpu.SemaphoreType.DMA((CHUNKS, 7)),
            pltpu.SemaphoreType.DMA,
        ],
        compiler_params=pltpu.CompilerParams(
            collective_id=1, has_side_effects=True, vmem_limit_bytes=24 << 20
        ),
        cost_estimate=pl.CostEstimate(flops=0, bytes_accessed=100_000_000, transcendentals=0),
        name="reduce_branch",
    )(clip_end, modulation, whole, part)


def per_device(
    tokens, queries, key_rows, value_rows, clip_ids, causal, modulation, w_mlp, w_attn_out, w_mlp_out
):
    local_rows = queries.shape[0]
    tp_size = lax.axis_size("tp")
    clips = causal.shape[0]
    numbers = jnp.arange(clips, dtype=jnp.int32)
    clip_end = jnp.sum((clip_ids[None, :] <= numbers[:, None]).astype(jnp.int32), axis=1)
    whole_rows, key_all, value_all, mlp_part = gather_rows(
        clip_end, modulation, tokens, key_rows, value_rows, w_mlp, w_mlp_out,
        lax.axis_size("ctx"), tp_size,
    )
    attended = attention(queries, key_all, value_all, jnp.concatenate([clip_end, causal]))
    part = jnp.dot(attended, w_attn_out, preferred_element_type=jnp.float32) + mlp_part
    return reduce_rows(clip_end, modulation, whole_rows, part.astype(jnp.bfloat16))


def solution(mesh):
    in_specs = (
        P("ctx", "tp"), P("ctx", "tp"), P("ctx", "tp"), P("ctx", "tp"),
        P(), P(), P(), P(None, "tp"), P("tp", None), P("tp", None),
    )
    out_specs = P(("ctx", "tp"), None)
    return jax.shard_map(
        per_device, mesh=mesh, in_specs=in_specs, out_specs=out_specs, check_vma=False
    )
```
